256 devices in a mesh: ctx: 32 (over x, z), head: 8 (over y, core).
Axes of the slice: x: 4, y: 4, z: 8, core: 2. Of those that a mesh axis runs over, the one named last changes fastest.
Arguments:
- queries: bfloat16 [65536, 128], P(('ctx', 'head')), may hold values from -6 to 6
- keys: bfloat16 [65536, 128], P(('ctx', 'head')), may hold values from -0.03125 to 0.03125
- values: bfloat16 [65536, 4096], P('ctx', 'head'), may hold values from -6 to 6
- tier_weight_rows: int32 [10, 65536], P(None, 'ctx'), may hold values from 0 to 15
- level_table: float32 [16, 32], P(None, 'head'), may hold values from 0.1 to 10
Outputs:
- mixed: bfloat16 [65536, 4096], P('ctx', 'head')
The draws below stay inside these ranges and needn't reach their ends.
All inputs are finite; a program needn't handle non-finite values.
Results may differ from the reference program's by a relative error of at most 0.0049.
Values may be sent and summed in bfloat16 or wider, within the bound.
A program may use at most 192 MiB of HBM per device.

```python
import math
import jax
import jax.numpy as jnp
from jax import lax

HEADS = 32
HEAD_DIM = 128
KEY_DIM = 128
GROUP = 128
CLASSES = 16
TOKENS = 65536
TIER_COUNT = 10


def set_ends(array, key, low, high):
    longest = array.shape.index(max(array.shape))
    spots = []
    for shift in (0, 1):
        where = [jax.random.randint(jax.random.fold_in(key, axis), (), 0, length) for axis, length in enumerate(array.shape)]
        where[longest] = (where[longest] + shift) % array.shape[longest]
        spots.append(tuple(where))
    return array.at[spots[0]].set(low).at[spots[1]].set(high)


def shard_levels(stream_key, dims, shards, smallest, high):
    factor_of = 1.0
    for dim, shards_of in shards:
        steps = jax.random.uniform(jax.random.fold_in(jax.random.fold_in(stream_key, 6), dim), (shards_of,), jnp.float32, smallest / len(shards), high / len(shards))
        factor_of = factor_of * jnp.repeat(jnp.exp(steps), dims[dim] // shards_of).reshape((-1,) + (1,) * (len(dims) - 1 - dim))
    return factor_of


def noise(stream_key, extent, spread, most, shards=(), held_as=jnp.bfloat16):
    drawn = jax.random.normal(stream_key, extent, jnp.float32) * spread
    if len(shards) > 0:
        drawn = shard_levels(stream_key, extent, shards, -0.22, 0.18) * drawn
    return jnp.clip(drawn, min=-most, max=most).astype(held_as)


def setup_inputs(seed: int = 0) -> dict:
    splits = jax.random.split(jax.random.key(seed), 6)
    return {
        "queries": noise(splits[0], (TOKENS, KEY_DIM), 1.0, 6.0, ((0, 256),)),
        "keys": noise(splits[1], (TOKENS, KEY_DIM), (TOKENS // 2) ** -0.5, 0.03125, ((0, 256),)),
        "values": noise(splits[2], (TOKENS, HEADS * HEAD_DIM), 1.0, 6.0, ((0, 32), (1, 8))),
        "tier_weight_rows": set_ends(jax.random.randint(splits[3], (TIER_COUNT, TOKENS), 0, CLASSES), jax.random.fold_in(splits[3], 1), 0, CLASSES - 1).astype(jnp.int32),
        "level_table": jnp.clip(jnp.exp(math.log(10.0) - 4.6051702 * jax.random.uniform(splits[4], (CLASSES, HEADS), jnp.float32) ** shard_levels(splits[4], (CLASSES, HEADS), ((1, 8),), -0.2, 0.2)), 0.1, 10.0),
    }


def reference(queries, keys, values, tier_weight_rows, level_table):
    weights = level_table[tier_weight_rows]
    share = weights / jnp.sum(weights, axis=0)
    query_f = queries.astype(jnp.float32)
    key_f = keys.astype(jnp.float32)
    groups = TOKENS // GROUP
    scores = jnp.einsum("nik,njk->nij", query_f.reshape(groups, GROUP, KEY_DIM), key_f.reshape(groups, GROUP, KEY_DIM))
    causal = jnp.tril(jnp.ones((GROUP, GROUP), dtype=bool))
    scores = jnp.where(causal[None], scores, 0.0).astype(jnp.bfloat16)
    score_f = scores.astype(jnp.float32)
    per_head = values.reshape(TOKENS, HEADS, HEAD_DIM).transpose(1, 0, 2)
    shared_key_head = share.transpose(2, 0, 1)

    def one_head(pair):
        head_vals, lam = pair
        value_f = head_vals.astype(jnp.float32)
        near = jnp.einsum("nij,njd->nid", score_f, value_f.reshape(groups, GROUP, HEAD_DIM)).reshape(TOKENS, HEAD_DIM)
        total = lam[0][:, None] * near
        for level in range(1, TIER_COUNT):
            half = GROUP * 2 ** (level - 1)
            blocks = TOKENS // (2 * half)
            grouped_probe_matrix = key_f.reshape(blocks, 2, half, KEY_DIM)
            grouped_content_matrix = value_f.reshape(blocks, 2, half, HEAD_DIM)
            query_blocked = query_f.reshape(blocks, 2, half, KEY_DIM)
            cumulative_memory = jnp.einsum("rlx,rlh->rxh", grouped_probe_matrix[:, 0], grouped_content_matrix[:, 0])
            cumulative_memory = lax.optimization_barrier(cumulative_memory.astype(jnp.bfloat16)).astype(jnp.float32)
            upper_half_branch = jnp.einsum("hfp,hpo->hfo", query_blocked[:, 1], cumulative_memory)
            part = jnp.stack([jnp.zeros_like(upper_half_branch), upper_half_branch], axis=1).reshape(TOKENS, HEAD_DIM)
            total = total + lam[level][:, None] * part
        return total.astype(jnp.bfloat16)

    outs = lax.map(one_head, (per_head, shared_key_head))
    return outs.transpose(1, 0, 2).reshape(TOKENS, HEADS * HEAD_DIM)
```

```python
import functools

import jax
import jax.numpy as jnp
from jax import lax
from jax.experimental import pallas as pl
from jax.experimental.pallas import tpu as pltpu
from jax.sharding import PartitionSpec as P

GROUP = 128
X, Y, Z = 4, 4, 8
CHUNK = 16
F32, BF16 = jnp.float32, jnp.bfloat16
DMA = pltpu.SemaphoreType.DMA


def nt(a, b):
    return lax.dot_general(a, b, (((1,), (1,)), ((), ())), preferred_element_type=F32)


def tn(a, b):
    return lax.dot_general(a, b, (((0,), (0,)), ((), ())), preferred_element_type=F32)


def nn(a, b):
    return jnp.dot(a, b, preferred_element_type=F32)


def kernel(
    q_in, k_in, v_in, rows_in, table_in, out,
    qbuf, kbuf, vbuf, rows, table, sh_t, sh, total, pairs, lev1, lev2, lev3, lev4,
    send, recv, pair6, half7, row_t, row_r, zst, xst, qs, obuf,
    loc_sem, v_sem, o_sem, gs_sem, gr_sem, as_sem, ar_sem, zs_sem, zr_sem,
    xs_sem, xr_sem, bs_sem, br_sem,
):
    ctx = lax.axis_index("ctx")
    head = lax.axis_index("head")
    x, z = ctx // Z, ctx % Z
    y, c = head // 2, head % 2
    sib = y * 2 + 1 - c
    up = ((y + 1) % Y) * 2 + c
    down = ((y + 3) % Y) * 2 + c
    far = ((y + 2) % Y) * 2 + c
    up_s, down_s, far_s = (((y + d) % Y) * 2 + 1 - c for d in (1, 3, 2))

    def remote(src, dst, ss, rs, ctx_to=ctx, head_to=head):
        return pltpu.make_async_remote_copy(
            src, dst, ss, rs, device_id=(ctx_to, head_to), device_id_type=pl.DeviceIdType.MESH
        )

    def z_at(d):
        return (z + d) % Z

    def ctx_z(d):
        return x * Z + z_at(d)

    copies = [
        pltpu.make_async_copy(rows_in, rows, loc_sem.at[0]),
        pltpu.make_async_copy(table_in, table, loc_sem.at[1]),
        pltpu.make_async_copy(k_in, kbuf.at[pl.ds(2 * head, 2)], loc_sem.at[2]),
        pltpu.make_async_copy(q_in, qbuf.at[pl.ds(2 * head, 2)], loc_sem.at[3]),
    ]
    for cp in copies:
        cp.start()
    v_copies = [
        pltpu.make_async_copy(v_in.at[pl.ds(2 * i, 2)], vbuf.at[pl.ds(2 * i, 2)], v_sem.at[i])
        for i in range(8)
    ]
    for cp in v_copies:
        cp.start()

    barrier = pltpu.get_barrier_semaphore()
    for d in range(1, 8):
        pl.semaphore_signal(
            barrier, 1, device_id=(ctx, (head + d) % 8), device_id_type=pl.DeviceIdType.MESH
        )
    for d in range(1, Z):
        pl.semaphore_signal(
            barrier, 1, device_id=(ctx_z(d), head), device_id_type=pl.DeviceIdType.MESH
        )
    for d in range(1, X):
        pl.semaphore_signal(
            barrier, 1, device_id=((x + d) % X * Z + z, head), device_id_type=pl.DeviceIdType.MESH
        )
    pl.semaphore_wait(barrier, 7 + 7 + 3)

    def gather(src, buf, n):
        def g(i, a, b, to):
            return remote(a, b, gs_sem.at[n, i], gr_sem.at[n, i], head_to=to)

        mine = buf.at[pl.ds(2 * head, 2)]
        s_down, s_up = buf.at[pl.ds(2 * down, 2)], buf.at[pl.ds(2 * up, 2)]
        far0, far1 = buf.at[pl.ds(2 * far, 1)], buf.at[pl.ds(2 * far + 1, 1)]
        d0, u1 = buf.at[pl.ds(2 * down, 1)], buf.at[pl.ds(2 * up + 1, 1)]
        return [
            g(0, src, mine, sib),
            g(1, src, mine, up),
            g(2, src, mine, down),
            g(3, s_down, s_down, sib),
            g(4, d0, d0, up),
            g(5, s_up, s_up, sib),
            g(6, u1, u1, down),
            g(7, far0, far0, sib),
            g(8, far1, far1, sib),
        ]

    gk = gather(k_in, kbuf, 0)
    gq = gather(q_in, qbuf, 1)
    for i in (1, 2, 0):
        gk[i].start()

    copies[0].wait()
    copies[1].wait()

    @pl.loop(0, 16)
    def _(g):
        r = rows[:, pl.ds(pl.multiple_of(g * GROUP, GROUP), GROUP)]
        ws = [jnp.zeros(r.shape, F32) for _ in range(4)]
        for cl in range(16):
            hit = r == cl
            ws = [jnp.where(hit, table[cl, h], w) for h, w in enumerate(ws)]
        for h, w in enumerate(ws):
            sh_t[pl.ds(16 * h, 10), :] = w / jnp.sum(w, axis=0, keepdims=True)
        sh[g] = sh_t[...].T

    gk[1].wait_recv()
    gk[4].start()
    gk[3].start()
    gk[2].wait_recv()
    gk[6].start()
    gk[5].start()
    for i in (1, 2, 0):
        gq[i].start()

    for cp in v_copies:
        cp.wait()

    def states(h):
        g0 = tn(kbuf[2 * h], vbuf[2 * h])
        g1 = tn(kbuf[2 * h + 1], vbuf[2 * h + 1])
        lev1[h] = g0.astype(BF16)
        pairs[h] = (g0 + g1).reshape(8, CHUNK, 512)

    copies[2].wait()
    states(head)
    gk[0].wait_recv()
    states(sib)
    states(down)
    states(up)
    gk[4].wait_recv()
    gk[7].start()
    gk[6].wait_recv()
    gk[8].start()
    gk[3].wait_recv()
    states(down_s)
    gk[5].wait_recv()
    states(up_s)
    states(far)
    gk[7].wait_recv()
    gk[8].wait_recv()
    states(far_s)

    a2a = [
        remote(send.at[z_at(d)], recv.at[z], as_sem.at[d], ar_sem.at[d], ctx_to=ctx_z(d))
        for d in range(1, Z)
    ]

    def chunk_state(j):
        p = [pairs[h, j] for h in range(8)]
        for i in range(4):
            lev2[i, j] = p[2 * i].astype(BF16)
        p4 = [p[2 * i] + p[2 * i + 1] for i in range(4)]
        lev3[0, j] = p4[0].astype(BF16)
        lev3[1, j] = p4[2].astype(BF16)
        low = p4[0] + p4[1]
        lev4[j] = low.astype(BF16)
        return (low + p4[2] + p4[3]).astype(BF16)

    for d in (4, 3, 5, 2, 6, 1, 7):
        j = z_at(d)
        send[j] = chunk_state(j)
        a2a[d - 1].start()
    recv[z] = chunk_state(z)

    gq[1].wait_recv()
    gq[4].start()
    gq[3].start()
    gq[2].wait_recv()
    gq[6].start()
    gq[5].start()
    gq[4].wait_recv()
    gq[7].start()
    gq[6].wait_recv()
    gq[8].start()
    copies[3].wait()
    for i in (0, 3, 5, 7, 8):
        gq[i].wait_recv()

    causal = lax.broadcasted_iota(jnp.int32, (GROUP, GROUP), 0) >= lax.broadcasted_iota(
        jnp.int32, (GROUP, GROUP), 1
    )

    def weighed(part, shares, level, h):
        lane = 16 * h + level
        return part[:, h * GROUP : (h + 1) * GROUP] * shares[:, lane : lane + 1]

    @pl.loop(0, 8)
    def _(i):
        for odd in range(2):
            g = 2 * i + odd
            q, shares = qbuf[g], sh[g]
            s = jnp.where(causal, nt(q, kbuf[g]), 0.0).astype(BF16)
            near = nn(s, vbuf[g])
            if odd:
                f1 = nn(q, lev1[i])
            for h in range(4):
                t = weighed(near, shares, 0, h)
                if odd:
                    t += weighed(f1, shares, 1, h)
                total[g, :, h * GROUP : (h + 1) * GROUP] = t

    def add_far(pair, state, level):
        g = pl.ds(2 * pair, 2)
        f = nn(qbuf[g].reshape(256, 128), state)
        shares = sh[g].reshape(256, 128)
        for h in range(4):
            cols = slice(h * GROUP, (h + 1) * GROUP)
            total[g, :, cols] += weighed(f, shares, level, h).reshape(2, GROUP, GROUP)

    @pl.loop(0, 4)
    def _(m):
        add_far(2 * m + 1, lev2[m].reshape(128, 512), 2)

    @pl.loop(0, 4)
    def _(m):
        add_far(4 * (m // 2) + 2 + m % 2, lev3[m // 2].reshape(128, 512), 3)

    for cp in a2a:
        cp.wait_recv()
    r = [recv[i].astype(F32) for i in range(8)]
    s01, s23, s45, s67 = (r[2 * i] + r[2 * i + 1] for i in range(4))
    s03 = s01 + s23
    row_t[...] = (s03 + s45 + s67).astype(BF16)

    xc = [
        remote(row_t, row_r.at[x], xs_sem.at[d], xr_sem.at[d], ctx_to=(x + d) % X * Z + z)
        for d in range(1, X)
    ]
    for d in range(1, X):

        @pl.when(x + d < X)
        def _():
            xc[d - 1].start()

    pair6[0] = s01.astype(BF16)
    pair6[1] = s45.astype(BF16)
    half7[...] = s03.astype(BF16)

    def z_copy(level, d):
        to = z_at(d)
        src = (recv.at[jnp.maximum(to - 1, 0)], pair6.at[to // 4], half7)[level]
        return remote(
            src, zst.at[level, z], zs_sem.at[level, d], zr_sem.at[level, d], ctx_to=ctx_z(d)
        )

    for level in (2, 1, 0):
        for d in (4, 3, 5, 2, 6, 1, 7):

            @pl.when((z_at(d) >> level) % 2 == 1)
            def _():
                z_copy(level, d).start()

    zst[0, z] = recv[jnp.maximum(z - 1, 0)]
    zst[1, z] = pair6[z // 4]
    zst[2, z] = half7[...]

    @pl.loop(0, 4)
    def _(m):
        add_far(4 + m, lev4[...].reshape(128, 512), 4)

    for d in range(1, X):

        @pl.when(x - d >= 0)
        def _():
            xc[d - 1].wait_recv()

    def b_copy(level, d):
        src = (row_r.at[jnp.maximum(x - 1, 0)], xst.at[1, z])[level]
        return remote(
            src, xst.at[level, z], bs_sem.at[level, d], br_sem.at[level, d], ctx_to=ctx_z(d)
        )

    def level_on(level):
        return (x >> level) % 2 == 1

    @pl.when(level_on(1))
    def _():
        xst[1, z] = (row_r[0].astype(F32) + row_r[1].astype(F32)).astype(BF16)
        for d in (4, 3, 5, 2, 6, 1, 7):
            b_copy(1, d).start()

    @pl.when(level_on(0))
    def _():
        xst[0, z] = row_r[x - 1]
        for d in (4, 3, 5, 2, 6, 1, 7):
            b_copy(0, d).start()

    for level in range(2):

        @pl.when(jnp.logical_not(level_on(level)))
        def _():
            xst[level] = jnp.zeros((8, CHUNK, 512), BF16)

    @pl.loop(0, 16)
    def _(g):
        q, shares = qbuf[g].astype(F32), sh[g]
        for h in range(4):
            for level in range(2):
                lane = 16 * h + 8 + level
                qs[h, g, :, level * 128 : (level + 1) * 128] = (
                    q * shares[:, lane : lane + 1]
                ).astype(BF16)

    for level in (2, 1, 0):

        @pl.when((z >> level) % 2 == 1)
        def _():
            for d in range(1, Z):
                z_copy(level, d).wait_recv()

            @pl.loop(0, 8)
            def _(m):
                add_far(m, zst[level].reshape(128, 512), 5 + level)

    for level in range(2):

        @pl.when(level_on(level))
        def _():
            for d in range(1, Z):
                b_copy(level, d).wait_recv()

    def o_copy(i):
        g = pl.ds(4 * i, 4)
        return pltpu.make_async_copy(obuf.at[g], out.at[g], o_sem.at[i])

    @pl.loop(0, 4)
    def _(i):
        g = pl.ds(4 * i, 4)
        for h in range(4):
            cols = slice(h * GROUP, (h + 1) * GROUP)
            f = nn(qs[h, g].reshape(512, 256), xst[:, :, :, cols].reshape(256, GROUP))
            obuf[g, :, cols] = (total[g, :, cols] + f.reshape(4, GROUP, GROUP)).astype(BF16)
        o_copy(i).start()

    for cp in gk + gq + a2a:
        cp.wait_send()
    for d in range(1, X):

        @pl.when(x + d < X)
        def _():
            xc[d - 1].wait_send()

    for level in range(3):
        for d in range(1, Z):

            @pl.when((z_at(d) >> level) % 2 == 1)
            def _():
                z_copy(level, d).wait_send()

    for level in range(2):

        @pl.when(level_on(level))
        def _():
            for d in range(1, Z):
                b_copy(level, d).wait_send()

    for i in range(4):
        o_copy(i).wait()


def local(queries, keys, values, tier_weight_rows, level_table):
    tokens, columns = values.shape
    groups = tokens // GROUP
    anywhere = pl.BlockSpec(memory_space=pl.ANY)
    vm = pltpu.VMEM
    out = pl.pallas_call(
        kernel,
        out_shape=jax.ShapeDtypeStruct((groups, GROUP, columns), BF16),
        in_specs=[anywhere] * 5,
        out_specs=anywhere,
        scratch_shapes=[
            vm((16, GROUP, 128), BF16),
            vm((16, GROUP, 128), BF16),
            vm((16, GROUP, 512), BF16),
            vm((10, 2048), jnp.int32),
            pltpu.SMEM((16, 4), F32),
            vm((GROUP, GROUP), F32),
            vm((16, GROUP, GROUP), F32),
            vm((16, GROUP, 512), F32),
            vm((8, 8, CHUNK, 512), F32),
            vm((8, 128, 512), BF16),
            vm((4, 8, CHUNK, 512), BF16),
            vm((2, 8, CHUNK, 512), BF16),
            vm((8, CHUNK, 512), BF16),
            vm((8, CHUNK, 512), BF16),
            vm((8, CHUNK, 512), BF16),
            vm((2, CHUNK, 512), BF16),
            vm((CHUNK, 512), BF16),
            vm((CHUNK, 512), BF16),
            vm((4, CHUNK, 512), BF16),
            vm((3, 8, CHUNK, 512), BF16),
            vm((2, 8, CHUNK, 512), BF16),
            vm((4, 16, GROUP, 256), BF16),
            vm((16, GROUP, 512), BF16),
            DMA((4,)),
            DMA((8,)),
            DMA((4,)),
            DMA((2, 9)),
            DMA((2, 9)),
            DMA((8,)),
            DMA((8,)),
            DMA((3, 8)),
            DMA((3, 8)),
            DMA((4,)),
            DMA((4,)),
            DMA((2, 8)),
            DMA((2, 8)),
        ],
        compiler_params=pltpu.CompilerParams(collective_id=0, has_side_effects=True),
    )(
        queries.reshape(2, GROUP, 128),
        keys.reshape(2, GROUP, 128),
        values.reshape(groups, GROUP, columns),
        tier_weight_rows,
        level_table,
    )
    return out.reshape(tokens, columns)


def solution(mesh):
    return jax.shard_map(
        local,
        mesh=mesh,
        in_specs=(
            P(("ctx", "head"), None),
            P(("ctx", "head"), None),
            P("ctx", "head"),
            P(None, "ctx"),
            P(None, "head"),
        ),
        out_specs=P("ctx", "head"),
        check_vma=False,
    )
```

```python
import functools

import jax
import jax.numpy as jnp
from jax import lax
from jax.experimental import pallas as pl
from jax.experimental.pallas import tpu as pltpu
from jax.sharding import PartitionSpec as P

GROUP = 128
X, Y, Z = 4, 4, 8
CHUNK = 64
F32, BF16 = jnp.float32, jnp.bfloat16
DMA = pltpu.SemaphoreType.DMA


def nt(a, b):
    return lax.dot_general(a, b, (((1,), (1,)), ((), ())), preferred_element_type=F32)


def nn(a, b):
    return jnp.dot(a, b, preferred_element_type=F32)


def kernel(
    q_in, k_in, v_in, rows_in, table_in, out,
    qbuf, kbuf, vbuf, vt, rows, table, sh, total, pairs, lev1, lev2, lev3, lev4,
    send, recv, pair6, half7, row_f, row_b, row_r, zst, xst, obuf,
    loc_sem, v_sem, o_sem, gs_sem, gr_sem, as_sem, ar_sem, zs_sem, zr_sem,
    xs_sem, xr_sem, bs_sem, br_sem,
):
    ctx = lax.axis_index("ctx")
    head = lax.axis_index("head")
    x, z = ctx // Z, ctx % Z
    y, c = head // 2, head % 2
    sib = y * 2 + 1 - c
    up = ((y + 1) % Y) * 2 + c
    down = ((y + 3) % Y) * 2 + c
    far = ((y + 2) % Y) * 2 + c
    up_s, down_s, far_s = (((y + d) % Y) * 2 + 1 - c for d in (1, 3, 2))

    def remote(src, dst, ss, rs, ctx_to=ctx, head_to=head):
        return pltpu.make_async_remote_copy(
            src, dst, ss, rs, device_id=(ctx_to, head_to), device_id_type=pl.DeviceIdType.MESH
        )

    def z_at(d):
        return (z + d) % Z

    def ctx_z(d):
        return x * Z + z_at(d)

    copies = [
        pltpu.make_async_copy(rows_in, rows, loc_sem.at[0]),
        pltpu.make_async_copy(table_in, table, loc_sem.at[1]),
        pltpu.make_async_copy(k_in, kbuf.at[pl.ds(2 * head, 2)], loc_sem.at[2]),
        pltpu.make_async_copy(q_in, qbuf.at[pl.ds(2 * head, 2)], loc_sem.at[3]),
    ]
    v_copies = [
        pltpu.make_async_copy(v_in.at[pl.ds(2 * i, 2)], vbuf.at[pl.ds(2 * i, 2)], v_sem.at[i])
        for i in range(8)
    ]

    barrier = pltpu.get_barrier_semaphore()
    partners = [(ctx, to) for to in (sib, up, down)]
    partners += [(ctx_z(d), head) for d in range(1, Z)]
    partners += [((x + d) % X * Z + z, head) for d in range(1, X)]
    for to in partners:
        pl.semaphore_signal(barrier, 1, device_id=to, device_id_type=pl.DeviceIdType.MESH)
    for cp in copies + v_copies:
        cp.start()
    pl.semaphore_wait(barrier, len(partners))

    def gather(src, buf, n):
        def g(i, a, b, to):
            return remote(a, b, gs_sem.at[n, i], gr_sem.at[n, i], head_to=to)

        mine = buf.at[pl.ds(2 * head, 2)]
        s_down, s_up = buf.at[pl.ds(2 * down, 2)], buf.at[pl.ds(2 * up, 2)]
        far0, far1 = buf.at[pl.ds(2 * far, 1)], buf.at[pl.ds(2 * far + 1, 1)]
        d0, u1 = buf.at[pl.ds(2 * down, 1)], buf.at[pl.ds(2 * up + 1, 1)]
        return [
            g(0, src, mine, sib),
            g(1, src, mine, up),
            g(2, src, mine, down),
            g(3, s_down, s_down, sib),
            g(4, d0, d0, up),
            g(5, s_up, s_up, sib),
            g(6, u1, u1, down),
            g(7, far0, far0, sib),
            g(8, far1, far1, sib),
        ]

    gk = gather(k_in, kbuf, 0)
    gq = gather(q_in, qbuf, 1)
    for i in (1, 2, 0):
        gk[i].start()

    for cp in v_copies:
        cp.wait()

    @pl.loop(0, 8)
    def _(i):
        for odd in range(2):
            vt[i, :, odd * 128 : (odd + 1) * 128] = vbuf[2 * i + odd].T

    gk[1].wait_recv()
    gk[4].start()
    gk[3].start()
    gk[2].wait_recv()
    gk[6].start()
    gk[5].start()
    for i in (1, 2, 0):
        gq[i].start()

    copies[0].wait()
    copies[1].wait()

    @pl.loop(0, 8)
    def _(i):
        r = rows[:, pl.ds(pl.multiple_of(i * 256, 256), 256)]
        ws = [jnp.zeros(r.shape, F32) for _ in range(4)]
        for cl in range(16):
            hit = r == cl
            ws = [jnp.where(hit, table[h, cl], w) for h, w in enumerate(ws)]
        for h, w in enumerate(ws):
            sh[i, pl.ds(16 * h, 10), :] = w / jnp.sum(w, axis=0, keepdims=True)


    def states(h):
        g0 = nn(vt[h, :, :128], kbuf[2 * h])
        g1 = nn(vt[h, :, 128:], kbuf[2 * h + 1])
        lev1[h] = g0.astype(BF16)
        pairs[h] = (g0 + g1).reshape(8, CHUNK, 128)

    copies[2].wait()
    states(head)
    gk[0].wait_recv()
    states(sib)
    states(down)
    states(up)
    gk[4].wait_recv()
    gk[7].start()
    gk[6].wait_recv()
    gk[8].start()
    gk[3].wait_recv()
    states(down_s)
    gk[5].wait_recv()
    states(up_s)
    states(far)
    gk[7].wait_recv()
    gk[8].wait_recv()
    states(far_s)

    a2a = [
        remote(send.at[z_at(d)], recv.at[z], as_sem.at[d], ar_sem.at[d], ctx_to=ctx_z(d))
        for d in range(1, Z)
    ]

    def chunk_state(j):
        p = [pairs[h, j] for h in range(8)]
        for i in range(4):
            lev2[i, j] = p[2 * i].astype(BF16)
        p4 = [p[2 * i] + p[2 * i + 1] for i in range(4)]
        lev3[0, j] = p4[0].astype(BF16)
        lev3[1, j] = p4[2].astype(BF16)
        low = p4[0] + p4[1]
        lev4[j] = low.astype(BF16)
        send[j] = (low + p4[2] + p4[3]).astype(BF16)

    for d in (4, 3, 5, 2, 6, 1, 7):
        chunk_state(z_at(d))
        a2a[d - 1].start()
    chunk_state(z)
    recv[z] = send[z]

    next_z = remote(send, zst.at[0], zs_sem.at[0, 0], zr_sem.at[0, 0], ctx_to=ctx_z(1))

    @pl.when(z % 2 == 0)
    def _():
        next_z.start()

    causal = lax.broadcasted_iota(jnp.int32, (GROUP, GROUP), 0) >= lax.broadcasted_iota(
        jnp.int32, (GROUP, GROUP), 1
    )
    heads = [slice(h * GROUP, (h + 1) * GROUP) for h in range(4)]

    def share(i, level, h):
        return sh[i, 16 * h + level : 16 * h + level + 1, :]

    def add_far(i, state, level):
        f = nt(state, qbuf[pl.ds(2 * i, 2)].reshape(256, 128))
        for h in range(4):
            total[i, heads[h], :] += f[heads[h]] * share(i, level, h)

    def near(i):
        for odd in range(2):
            g = 2 * i + odd
            cols = slice(odd * GROUP, (odd + 1) * GROUP)
            q = qbuf[g]
            s = jnp.where(causal, nt(q, kbuf[g]), 0.0).astype(BF16)
            f0 = nt(vt[i, :, cols], s)
            if odd:
                f1 = nt(lev1[i], q)
            for h in range(4):
                t = f0[heads[h]] * share(i, 0, h)[:, cols]
                if odd:
                    t += f1[heads[h]] * share(i, 1, h)[:, cols]
                total[i, heads[h], cols] = t

        @pl.when(i % 2 == 1)
        def _():
            add_far(i, lev2[i // 2].reshape(512, 128), 2)

        @pl.when(i // 2 % 2 == 1)
        def _():
            add_far(i, lev3[i // 4].reshape(512, 128), 3)

        @pl.when(i // 4 == 1)
        def _():
            add_far(i, lev4[...].reshape(512, 128), 4)

    copies[3].wait()
    near(head)
    gq[1].wait_recv()
    gq[4].start()
    gq[3].start()
    gq[2].wait_recv()
    gq[6].start()
    gq[5].start()
    gq[0].wait_recv()
    near(sib)

    @pl.loop(0, 2)
    def _(e):
        near((y + 3 + 2 * e) % Y * 2 + c)

    gq[4].wait_recv()
    gq[7].start()
    gq[6].wait_recv()
    gq[8].start()

    for cp in a2a:
        cp.wait_recv()
    r = [recv[i].astype(F32) for i in range(8)]
    s01, s23, s45, s67 = (r[2 * i] + r[2 * i + 1] for i in range(4))
    s03 = s01 + s23
    row = s03 + s45 + s67
    row_f[...] = row

    def x_copy(to):
        return remote(row_f, row_r.at[x], xs_sem.at[to], xr_sem.at[x], ctx_to=to * Z + z)

    @pl.when(x < 2)
    def _():
        for to in (2, 3):
            x_copy(to).start()

    row_b[...] = row.astype(BF16)
    pair6[0] = s01.astype(BF16)
    pair6[1] = s45.astype(BF16)
    half7[...] = s03.astype(BF16)

    def t_copy(d):
        to = (x + 1) % X * Z + z_at(d)
        return remote(row_b, xst.at[0, z], bs_sem.at[0, d], br_sem.at[0, d], ctx_to=to)

    def z_copy(level, d):
        src = (None, pair6.at[z_at(d) // 4], half7)[level]
        return remote(
            src, zst.at[level, z], zs_sem.at[level, d], zr_sem.at[level, d], ctx_to=ctx_z(d)
        )

    order = (4, 3, 5, 2, 6, 1, 7)
    for level in (2, 1):
        for d in order:

            @pl.when((z_at(d) >> level) % 2 == 1)
            def _():
                z_copy(level, d).start()

    @pl.when(x % 2 == 0)
    def _():
        for d in order + (0,):
            t_copy(d).start()

    zst[1, z] = pair6[z // 4]
    zst[2, z] = half7[...]

    gq[3].wait_recv()
    gq[5].wait_recv()

    @pl.loop(0, 2)
    def _(e):
        near((y + 3 + 2 * e) % Y * 2 + 1 - c)

    def b_copy(d):
        return remote(
            xst.at[1, z], xst.at[1, z], bs_sem.at[1, d], br_sem.at[1, d], ctx_to=ctx_z(d)
        )

    @pl.when(x >= 2)
    def _():
        for s in range(2):
            remote(row_f, row_r.at[s], xs_sem.at[s], xr_sem.at[s]).wait_recv()
        xst[1, z] = (row_r[0] + row_r[1]).astype(BF16)
        for d in order:
            b_copy(d).start()

    @pl.when(x < 2)
    def _():
        xst[1] = jnp.zeros((8, CHUNK, 128), BF16)

    @pl.when(x % 2 == 0)
    def _():
        xst[0] = jnp.zeros((8, CHUNK, 128), BF16)

    gq[7].wait_recv()
    gq[8].wait_recv()

    @pl.loop(0, 2)
    def _(e):
        near((y + 2) % Y * 2 + e)

    @pl.when(z % 2 == 1)
    def _():
        next_z.wait_recv()

        @pl.loop(0, 8)
        def _(m):
            add_far(m, zst[0].reshape(512, 128), 5)

    for level in (2, 1):

        @pl.when((z >> level) % 2 == 1)
        def _():
            for d in range(1, Z):
                z_copy(level, d).wait_recv()

            @pl.loop(0, 8)
            def _(m):
                add_far(m, zst[level].reshape(512, 128), 5 + level)

    @pl.when(x % 2 == 1)
    def _():
        for d in range(Z):
            t_copy(d).wait_recv()

    @pl.when(x >= 2)
    def _():
        for d in range(1, Z):
            b_copy(d).wait_recv()

    def o_copy(i):
        g = pl.ds(2 * i, 2)
        return pltpu.make_async_copy(obuf.at[g], out.at[g], o_sem.at[i])

    @pl.loop(0, 8)
    def _(i):
        q = qbuf[pl.ds(2 * i, 2)].reshape(256, 128)
        f8 = nt(xst[0].reshape(512, 128), q)
        f9 = nt(xst[1].reshape(512, 128), q)
        for h in range(4):
            t = total[i, heads[h], :] + f8[heads[h]] * share(i, 8, h) + f9[heads[h]] * share(i, 9, h)
            obuf[pl.ds(2 * i, 2), :, heads[h]] = t.astype(BF16).T.reshape(2, GROUP, GROUP)
        o_copy(i).start()

    for cp in gk + gq + a2a:
        cp.wait_send()

    @pl.when(z % 2 == 0)
    def _():
        next_z.wait_send()

    @pl.when(x < 2)
    def _():
        for to in (2, 3):
            x_copy(to).wait_send()

    for level in (2, 1):
        for d in range(1, Z):

            @pl.when((z_at(d) >> level) % 2 == 1)
            def _():
                z_copy(level, d).wait_send()

    @pl.when(x % 2 == 0)
    def _():
        for d in range(Z):
            t_copy(d).wait_send()

    @pl.when(x >= 2)
    def _():
        for d in range(1, Z):
            b_copy(d).wait_send()

    for i in range(8):
        o_copy(i).wait()


def local(queries, keys, values, tier_weight_rows, level_table):
    tokens, columns = values.shape
    groups = tokens // GROUP
    anywhere = pl.BlockSpec(memory_space=pl.ANY)
    vm = pltpu.VMEM
    out = pl.pallas_call(
        kernel,
        out_shape=jax.ShapeDtypeStruct((groups, GROUP, columns), BF16),
        in_specs=[anywhere] * 5,
        out_specs=anywhere,
        scratch_shapes=[
            vm((16, GROUP, 128), BF16),
            vm((16, GROUP, 128), BF16),
            vm((16, GROUP, 512), BF16),
            vm((8, 512, 256), BF16),
            vm((10, 2048), jnp.int32),
            pltpu.SMEM((4, 16), F32),
            vm((8, 64, 256), F32),
            vm((8, 512, 256), F32),
            vm((8, 8, CHUNK, 128), F32),
            vm((8, 512, 128), BF16),
            vm((4, 8, CHUNK, 128), BF16),
            vm((2, 8, CHUNK, 128), BF16),
            vm((8, CHUNK, 128), BF16),
            vm((8, CHUNK, 128), BF16),
            vm((8, CHUNK, 128), BF16),
            vm((2, CHUNK, 128), BF16),
            vm((CHUNK, 128), BF16),
            vm((CHUNK, 128), F32),
            vm((CHUNK, 128), BF16),
            vm((2, CHUNK, 128), F32),
            vm((3, 8, CHUNK, 128), BF16),
            vm((2, 8, CHUNK, 128), BF16),
            vm((16, GROUP, 512), BF16),
            DMA((4,)),
            DMA((8,)),
            DMA((8,)),
            DMA((2, 9)),
            DMA((2, 9)),
            DMA((8,)),
            DMA((8,)),
            DMA((3, 8)),
            DMA((3, 8)),
            DMA((4,)),
            DMA((2,)),
            DMA((2, 8)),
            DMA((2, 8)),
        ],
        compiler_params=pltpu.CompilerParams(collective_id=0, has_side_effects=True),
    )(
        queries.reshape(2, GROUP, 128),
        keys.reshape(2, GROUP, 128),
        values.reshape(groups, GROUP, columns),
        tier_weight_rows,
        level_table.T,
    )
    return out.reshape(tokens, columns)


def solution(mesh):
    return jax.shard_map(
        local,
        mesh=mesh,
        in_specs=(
            P(("ctx", "head"), None),
            P(("ctx", "head"), None),
            P("ctx", "head"),
            P(None, "ctx"),
            P(None, "head"),
        ),
        out_specs=P("ctx", "head"),
        check_vma=False,
    )
```

```python
import functools

import jax
import jax.numpy as jnp
from jax import lax
from jax.experimental import pallas as pl
from jax.experimental.pallas import tpu as pltpu
from jax.sharding import PartitionSpec as P

GROUP = 128
X, Y, Z = 4, 4, 8
CHUNK = 64
F32, BF16 = jnp.float32, jnp.bfloat16
DMA = pltpu.SemaphoreType.DMA


def nt(a, b):
    return lax.dot_general(a, b, (((1,), (1,)), ((), ())), preferred_element_type=F32)


def nn(a, b):
    return jnp.dot(a, b, preferred_element_type=F32)


def kernel(
    q_in, k_in, v_in, rows_in, table_in,
    qbuf, sh, total, xst,
    kbuf, vbuf, vt, rows, table, pairs, lev1, lev2, lev3, lev4,
    send, recv, pair6, half7, row_f, row_b, row_r, both, zst,
    loc_sem, v_sem, gs_sem, gr_sem, as_sem, ar_sem, zs_sem, zr_sem,
    xs_sem, xr_sem, bs_sem, br_sem, in_sem,
):
    ctx = lax.axis_index("ctx")
    head = lax.axis_index("head")
    x, z = ctx // Z, ctx % Z
    y, c = head // 2, head % 2
    sib = y * 2 + 1 - c
    up = ((y + 1) % Y) * 2 + c
    down = ((y + 3) % Y) * 2 + c
    far = ((y + 2) % Y) * 2 + c
    up_s, down_s, far_s = (((y + d) % Y) * 2 + 1 - c for d in (1, 3, 2))

    def remote(src, dst, ss, rs, ctx_to=ctx, head_to=head):
        return pltpu.make_async_remote_copy(
            src, dst, ss, rs, device_id=(ctx_to, head_to), device_id_type=pl.DeviceIdType.MESH
        )

    def z_at(d):
        return (z + d) % Z

    def ctx_z(d):
        return x * Z + z_at(d)

    copies = [
        pltpu.make_async_copy(rows_in, rows, loc_sem.at[0]),
        pltpu.make_async_copy(table_in, table, loc_sem.at[1]),
        pltpu.make_async_copy(k_in, kbuf.at[pl.ds(2 * head, 2)], loc_sem.at[2]),
        pltpu.make_async_copy(q_in, qbuf.at[pl.ds(2 * head, 2)], loc_sem.at[3]),
    ]
    v_copies = [
        pltpu.make_async_copy(v_in.at[pl.ds(2 * i, 2)], vbuf.at[pl.ds(2 * i, 2)], v_sem.at[i])
        for i in range(8)
    ]

    mesh_id = pl.DeviceIdType.MESH
    barrier = pltpu.get_barrier_semaphore()
    next_x = [((x + d) % X * Z + z, head) for d in (1, X - 1)]
    next_z = [(ctx_z(d), head) for d in (1, Z - 1)]
    partners = [(ctx, to) for to in (sib, up, down)] + next_z + next_x
    for to in partners:
        pl.semaphore_signal(barrier, 1, device_id=to, device_id_type=mesh_id)
    for cp in copies + v_copies:
        cp.start()
    pl.semaphore_wait(barrier, len(partners))

    def gather(src, buf, n):
        def g(i, a, b, to):
            return remote(a, b, gs_sem.at[n, i], gr_sem.at[n, i], head_to=to)

        def part(h, half):
            return buf.at[pl.ds(2 * h + half, 1)]

        def whole(h):
            return buf.at[pl.ds(2 * h, 2)]

        first, second = src.at[pl.ds(0, 1)], src.at[pl.ds(1, 1)]
        return [
            g(0, src, whole(head), sib),
            g(1, first, part(head, 0), up),
            g(2, second, part(head, 1), up),
            g(3, second, part(head, 1), down),
            g(4, first, part(head, 0), down),
            g(5, part(down, 0), part(down, 0), up),
            g(6, part(up, 1), part(up, 1), down),
            g(7, whole(down), whole(down), sib),
            g(8, whole(up), whole(up), sib),
            g(9, part(far, 0), part(far, 0), sib),
            g(10, part(far, 1), part(far, 1), sib),
        ]

    def step(copies, *pairs):
        for landed, started in pairs:
            copies[landed].wait_recv()
            copies[started].start()

    gk = gather(k_in, kbuf, 0)
    gq = gather(q_in, qbuf, 1)
    for i in (1, 3, 2, 4, 0):
        gk[i].start()
    for to in next_z + next_x:
        pl.semaphore_signal(in_sem.at[0], 1, device_id=to, device_id_type=mesh_id)

    for cp in v_copies:
        cp.wait()

    @pl.loop(0, 8)
    def _(i):
        for odd in range(2):
            vt[i, :, odd * 128 : (odd + 1) * 128] = vbuf[2 * i + odd].T

    copies[0].wait()
    copies[1].wait()

    @pl.loop(0, 8)
    def _(i):
        r = rows[:, pl.ds(pl.multiple_of(i * 256, 256), 256)]
        ws = [jnp.zeros(r.shape, F32) for _ in range(4)]
        for cl in range(16):
            hit = r == cl
            ws = [jnp.where(hit, table[h, cl], w) for h, w in enumerate(ws)]
        for h, w in enumerate(ws):
            sh[i, pl.ds(16 * h, 10), :] = w / jnp.sum(w, axis=0, keepdims=True)

    pl.semaphore_wait(in_sem.at[0], 4)
    for d in (2, Z - 2):
        pl.semaphore_signal(
            in_sem.at[1], 1, device_id=(ctx_z(d), head), device_id_type=mesh_id
        )

    step(gk, (1, 5), (3, 6), (2, 7), (4, 8))
    for i in (1, 3, 2, 4):
        gq[i].start()


    def states(h):
        g0 = nn(vt[h, :, :128], kbuf[2 * h])
        g1 = nn(vt[h, :, 128:], kbuf[2 * h + 1])
        lev1[h] = g0.astype(BF16)
        pairs[h] = (g0 + g1).reshape(8, CHUNK, 128)

    copies[2].wait()
    states(head)
    states(down)
    states(up)
    step(gk, (5, 9), (6, 10))
    gq[0].start()
    states(far)
    gk[0].wait_recv()
    states(sib)
    gk[7].wait_recv()
    states(down_s)
    gk[8].wait_recv()
    states(up_s)
    gk[9].wait_recv()
    gk[10].wait_recv()
    states(far_s)
    pl.semaphore_wait(in_sem.at[1], 2)

    a2a = [
        remote(send.at[z_at(d)], recv.at[z], as_sem.at[d], ar_sem.at[d], ctx_to=ctx_z(d))
        for d in range(1, Z)
    ]

    def chunk_state(j):
        p = [pairs[h, j] for h in range(8)]
        for i in range(4):
            lev2[i, j] = p[2 * i].astype(BF16)
        p4 = [p[2 * i] + p[2 * i + 1] for i in range(4)]
        lev3[0, j] = p4[0].astype(BF16)
        lev3[1, j] = p4[2].astype(BF16)
        low = p4[0] + p4[1]
        lev4[j] = low.astype(BF16)
        send[j] = (low + p4[2] + p4[3]).astype(BF16)

    for d in (4, 3, 5, 2, 6, 1, 7):
        chunk_state(z_at(d))
        a2a[d - 1].start()
    chunk_state(z)
    recv[z] = send[z]

    z_next = remote(send, zst.at[0], zs_sem.at[0, 0], zr_sem.at[0, 0], ctx_to=ctx_z(1))

    @pl.when(z % 2 == 0)
    def _():
        z_next.start()

    causal = lax.broadcasted_iota(jnp.int32, (GROUP, GROUP), 0) >= lax.broadcasted_iota(
        jnp.int32, (GROUP, GROUP), 1
    )
    heads = [slice(h * GROUP, (h + 1) * GROUP) for h in range(4)]

    def share(i, level, h):
        return sh[i, 16 * h + level : 16 * h + level + 1, :]

    def add_far(i, state, level):
        f = nt(state, qbuf[pl.ds(2 * i, 2)].reshape(256, 128))
        for h in range(4):
            total[i, heads[h], :] += f[heads[h]] * share(i, level, h)

    def near(i):
        for odd in range(2):
            g = 2 * i + odd
            cols = slice(odd * GROUP, (odd + 1) * GROUP)
            q = qbuf[g]
            s = jnp.where(causal, nt(q, kbuf[g]), 0.0).astype(BF16)
            f0 = nt(vt[i, :, cols], s)
            if odd:
                f1 = nt(lev1[i], q)
            for h in range(4):
                t = f0[heads[h]] * share(i, 0, h)[:, cols]
                if odd:
                    t += f1[heads[h]] * share(i, 1, h)[:, cols]
                total[i, heads[h], cols] = t

        @pl.when(i % 2 == 1)
        def _():
            add_far(i, lev2[i // 2].reshape(512, 128), 2)

        @pl.when(i // 2 % 2 == 1)
        def _():
            add_far(i, lev3[i // 4].reshape(512, 128), 3)

        @pl.when(i // 4 == 1)
        def _():
            add_far(i, lev4[...].reshape(512, 128), 4)

    copies[3].wait()
    near(head)
    step(gq, (1, 5), (3, 6), (2, 7), (4, 8))
    gq[0].wait_recv()
    near(sib)

    @pl.loop(0, 2)
    def _(e):
        near((y + 3 + 2 * e) % Y * 2 + c)

    step(gq, (5, 9), (6, 10))

    for cp in a2a:
        cp.wait_recv()
    r = [recv[i].astype(F32) for i in range(8)]
    s01, s23, s45, s67 = (r[2 * i] + r[2 * i + 1] for i in range(4))
    s03 = s01 + s23
    row = s03 + s45 + s67
    row_f[...] = row

    def x_copy(to):
        return remote(row_f, row_r.at[x], xs_sem.at[to], xr_sem.at[x], ctx_to=to * Z + z)

    for to, sender in ((3, x < 2), (1, x == 0)):

        @pl.when(sender)
        def _():
            x_copy(to).start()

    row_b[...] = row.astype(BF16)
    pair6[0] = s01.astype(BF16)
    pair6[1] = s45.astype(BF16)
    half7[...] = s03.astype(BF16)

    def t_copy(d):
        to = (x + 1) % X * Z + z_at(d)
        return remote(row_b, xst.at[0, z], bs_sem.at[0, d], br_sem.at[0, d], ctx_to=to)

    def z_copy(level, d):
        src = (None, pair6.at[z_at(d) // 4], half7)[level]
        return remote(
            src, zst.at[level, z], zs_sem.at[level, d], zr_sem.at[level, d], ctx_to=ctx_z(d)
        )

    order = (4, 3, 5, 2, 6, 1, 7)
    for level in (2, 1):
        for d in order:

            @pl.when((z_at(d) >> level) % 2 == 1)
            def _():
                z_copy(level, d).start()

    @pl.when(x % 2 == 0)
    def _():
        for d in order + (0,):
            t_copy(d).start()

    zst[1, z] = pair6[z // 4]
    zst[2, z] = half7[...]

    gq[7].wait_recv()
    gq[8].wait_recv()

    @pl.loop(0, 2)
    def _(e):
        near((y + 3 + 2 * e) % Y * 2 + 1 - c)

    def b_copy(d):
        to = jnp.where(x == 1, ctx_z(d) + Z, ctx_z(d))
        return remote(both, xst.at[1, z], bs_sem.at[1, d], br_sem.at[1, d], ctx_to=to)

    def x_wait(s):
        remote(row_f, row_r.at[s], xs_sem.at[s], xr_sem.at[s]).wait_recv()

    @pl.when(x == 1)
    def _():
        x_wait(0)
        both[...] = (row_r[0] + row_f[...]).astype(BF16)
        for d in order + (0,):
            b_copy(d).start()

    @pl.when(x == 3)
    def _():
        x_wait(0)
        x_wait(1)
        t = (row_r[0] + row_r[1]).astype(BF16)
        both[...] = t
        xst[1, z] = t
        for d in order:
            b_copy(d).start()

    @pl.when(x < 2)
    def _():
        xst[1] = jnp.zeros((8, CHUNK, 128), BF16)

    gq[9].wait_recv()
    gq[10].wait_recv()

    @pl.loop(0, 2)
    def _(e):
        near((y + 2) % Y * 2 + e)

    def add_all(state, level):
        @pl.loop(0, 4)
        def _(m):
            for i in range(2):
                add_far(2 * m + i, state.reshape(512, 128), level)

    @pl.when(z % 2 == 1)
    def _():
        z_next.wait_recv()
        add_all(zst[0], 5)

    for level in (2, 1):
        @pl.when((z >> level) % 2 == 1)
        def _():
            for d in range(1, Z):
                z_copy(level, d).wait_recv()
            add_all(zst[level], 5 + level)

    @pl.when(x % 2 == 1)
    def _():
        for d in range(Z):
            t_copy(d).wait_recv()
        add_all(xst[0], 8)

    @pl.when(x >= 2)
    def _():
        for d in range(1, Z):
            b_copy(d).wait_recv()

    @pl.when(x == 2)
    def _():
        b_copy(0).wait_recv()

    for cp in gk + gq + a2a:
        cp.wait_send()

    @pl.when(z % 2 == 0)
    def _():
        z_next.wait_send()

    for to, sender in ((3, x < 2), (1, x == 0)):

        @pl.when(sender)
        def _():
            x_copy(to).wait_send()

    for level in (2, 1):
        for d in range(1, Z):

            @pl.when((z_at(d) >> level) % 2 == 1)
            def _():
                z_copy(level, d).wait_send()

    @pl.when(x % 2 == 0)
    def _():
        for d in range(Z):
            t_copy(d).wait_send()

    @pl.when(x % 2 == 1)
    def _():
        for d in range(1, Z):
            b_copy(d).wait_send()

    @pl.when(x == 1)
    def _():
        b_copy(0).wait_send()


def finish(qbuf, sh, total, xst, out, obuf, o_sem):
    def o_copy(m):
        g = pl.ds(4 * m, 4)
        return pltpu.make_async_copy(obuf.at[g], out.at[g], o_sem.at[m])

    @pl.loop(0, 4)
    def _(m):
        for i in (2 * m, 2 * m + 1):
            f = nt(xst[1].reshape(512, 128), qbuf[pl.ds(2 * i, 2)].reshape(256, 128))
            for h in range(4):
                rows = slice(h * GROUP, (h + 1) * GROUP)
                lane = 16 * h + 9
                t = total[i, rows, :] + f[rows] * sh[i, lane : lane + 1, :]
                obuf[pl.ds(2 * i, 2), :, rows] = t.astype(BF16).T.reshape(2, GROUP, GROUP)
        o_copy(m).start()

    for m in range(4):
        o_copy(m).wait()


def local(queries, keys, values, tier_weight_rows, level_table):
    tokens, columns = values.shape
    groups = tokens // GROUP
    anywhere = pl.BlockSpec(memory_space=pl.ANY)
    vm = pltpu.VMEM
    kept = (
        vm((16, GROUP, 128), BF16),
        vm((8, 64, 256), F32),
        vm((8, 512, 256), F32),
        vm((2, 8, CHUNK, 128), BF16),
    )
    in_vmem = [pl.BlockSpec(memory_space=pltpu.VMEM)] * len(kept)
    parts = pl.pallas_call(
        kernel,
        out_shape=kept,
        in_specs=[pl.BlockSpec(memory_space=pltpu.MemorySpace.HBM)] * 5,
        out_specs=in_vmem,
        scratch_shapes=[
            vm((16, GROUP, 128), BF16),
            vm((16, GROUP, 512), BF16),
            vm((8, 512, 256), BF16),
            vm((10, 2048), jnp.int32),
            pltpu.SMEM((4, 16), F32),
            vm((8, 8, CHUNK, 128), F32),
            vm((8, 512, 128), BF16),
            vm((4, 8, CHUNK, 128), BF16),
            vm((2, 8, CHUNK, 128), BF16),
            vm((8, CHUNK, 128), BF16),
            vm((8, CHUNK, 128), BF16),
            vm((8, CHUNK, 128), BF16),
            vm((2, CHUNK, 128), BF16),
            vm((CHUNK, 128), BF16),
            vm((CHUNK, 128), F32),
            vm((CHUNK, 128), BF16),
            vm((2, CHUNK, 128), F32),
            vm((CHUNK, 128), BF16),
            vm((3, 8, CHUNK, 128), BF16),
            DMA((4,)),
            DMA((8,)),
            DMA((2, 11)),
            DMA((2, 11)),
            DMA((8,)),
            DMA((8,)),
            DMA((3, 8)),
            DMA((3, 8)),
            DMA((4,)),
            DMA((2,)),
            DMA((2, 8)),
            DMA((2, 8)),
            pltpu.SemaphoreType.REGULAR((2,)),
        ],
        compiler_params=pltpu.CompilerParams(
            collective_id=0, has_side_effects=True, vmem_limit_bytes=24 * 2**20
        ),
    )(*(
        pltpu.with_memory_space_constraint(arg, pltpu.MemorySpace.HBM)
        for arg in (
            queries.reshape(2, GROUP, 128),
            keys.reshape(2, GROUP, 128),
            values.reshape(groups, GROUP, columns),
            tier_weight_rows,
            level_table.T,
        )
    ))
    out = pl.pallas_call(
        finish,
        out_shape=jax.ShapeDtypeStruct((groups, GROUP, columns), BF16),
        in_specs=in_vmem,
        out_specs=anywhere,
        scratch_shapes=[vm((groups, GROUP, columns), BF16), DMA((4,))],
        compiler_params=pltpu.CompilerParams(vmem_limit_bytes=12 * 2**20),
    )(*parts)
    return out.reshape(tokens, columns)


def solution(mesh):
    return jax.shard_map(
        local,
        mesh=mesh,
        in_specs=(
            P(("ctx", "head"), None),
            P(("ctx", "head"), None),
            P("ctx", "head"),
            P(None, "ctx"),
            P(None, "head"),
        ),
        out_specs=P("ctx", "head"),
        check_vma=False,
    )
```

```python
import functools

import jax
import jax.numpy as jnp
from jax import lax
from jax.experimental import pallas as pl
from jax.experimental.pallas import tpu as pltpu
from jax.sharding import PartitionSpec as P

GROUP = 128
X, Y, Z = 4, 4, 8
CHUNK = 64
F32, BF16 = jnp.float32, jnp.bfloat16
DMA = pltpu.SemaphoreType.DMA


def nt(a, b):
    return lax.dot_general(a, b, (((1,), (1,)), ((), ())), preferred_element_type=F32)


def nn(a, b):
    return jnp.dot(a, b, preferred_element_type=F32)


def kernel(
    q_in, k_in, v_in, rows_in, table_in,
    qbuf, sh, total, xst,
    kbuf, vbuf, vt, rows, table, pairs, lev1, lev2, lev3, lev4,
    send, recv, pair6, half7, row_f, row_b, row_r, both, zst,
    loc_sem, v_sem, gs_sem, gr_sem, as_sem, ar_sem, zs_sem, zr_sem,
    xs_sem, xr_sem, bs_sem, br_sem, in_sem,
):
    ctx = lax.axis_index("ctx")
    head = lax.axis_index("head")
    x, z = ctx // Z, ctx % Z
    y, c = head // 2, head % 2
    sib = y * 2 + 1 - c
    up = ((y + 1) % Y) * 2 + c
    down = ((y + 3) % Y) * 2 + c
    far = ((y + 2) % Y) * 2 + c
    up_s, down_s, far_s = (((y + d) % Y) * 2 + 1 - c for d in (1, 3, 2))

    def remote(src, dst, ss, rs, ctx_to=ctx, head_to=head):
        return pltpu.make_async_remote_copy(
            src, dst, ss, rs, device_id=(ctx_to, head_to), device_id_type=pl.DeviceIdType.MESH
        )

    def z_at(d):
        return (z + d) % Z

    def ctx_z(d):
        return x * Z + z_at(d)

    copies = [
        pltpu.make_async_copy(rows_in, rows, loc_sem.at[0]),
        pltpu.make_async_copy(table_in, table, loc_sem.at[1]),
        pltpu.make_async_copy(k_in, kbuf.at[pl.ds(2 * head, 2)], loc_sem.at[2]),
        pltpu.make_async_copy(q_in, qbuf.at[pl.ds(2 * head, 2)], loc_sem.at[3]),
    ]
    v_copies = [
        pltpu.make_async_copy(v_in.at[pl.ds(2 * i, 2)], vbuf.at[pl.ds(2 * i, 2)], v_sem.at[i])
        for i in range(8)
    ]

    mesh_id = pl.DeviceIdType.MESH
    barrier = pltpu.get_barrier_semaphore()
    next_x = [((x + d) % X * Z + z, head) for d in (1, X - 1)]
    next_z = [(ctx_z(d), head) for d in (1, Z - 1)]
    partners = [(ctx, to) for to in (sib, up, down, far)] + next_z + next_x
    for to in partners:
        pl.semaphore_signal(barrier, 1, device_id=to, device_id_type=mesh_id)
    for cp in copies + v_copies:
        cp.start()
    pl.semaphore_wait(barrier, len(partners))

    def gather(src, buf, n):
        def g(i, a, b, to):
            return remote(a, b, gs_sem.at[n, i], gr_sem.at[n, i], head_to=to)

        def shard(h):
            return buf.at[pl.ds(2 * h, 2)]

        return [
            g(0, src, shard(head), sib),
            g(1, src, shard(head), up),
            g(2, src, shard(head), down),
            g(3, src, shard(head), far),
            g(4, shard(down), shard(down), sib),
            g(5, shard(up), shard(up), sib),
            g(6, shard(far), shard(far), sib),
        ]

    def step(copies, *pairs):
        for landed, started in pairs:
            copies[landed].wait_recv()
            copies[started].start()

    gk = gather(k_in, kbuf, 0)
    gq = gather(q_in, qbuf, 1)
    for i in (3, 1, 2, 0):
        gk[i].start()
    for to in next_z + next_x:
        pl.semaphore_signal(in_sem.at[0], 1, device_id=to, device_id_type=mesh_id)

    for cp in v_copies:
        cp.wait()

    @pl.loop(0, 8)
    def _(i):
        for odd in range(2):
            vt[i, :, odd * 128 : (odd + 1) * 128] = vbuf[2 * i + odd].T

    copies[0].wait()
    copies[1].wait()

    @pl.loop(0, 8)
    def _(i):
        r = rows[:, pl.ds(pl.multiple_of(i * 256, 256), 256)]
        ws = [jnp.zeros(r.shape, F32) for _ in range(4)]
        for cl in range(16):
            hit = r == cl
            ws = [jnp.where(hit, table[h, cl], w) for h, w in enumerate(ws)]
        for h, w in enumerate(ws):
            sh[i, pl.ds(16 * h, 10), :] = w / jnp.sum(w, axis=0, keepdims=True)

    pl.semaphore_wait(in_sem.at[0], 4)
    for d in (2, Z - 2):
        pl.semaphore_signal(
            in_sem.at[1], 1, device_id=(ctx_z(d), head), device_id_type=mesh_id
        )

    step(gk, (1, 4), (2, 5))
    for i in (3, 1, 2):
        gq[i].start()


    def states(h):
        g0 = nn(vt[h, :, :128], kbuf[2 * h])
        g1 = nn(vt[h, :, 128:], kbuf[2 * h + 1])
        lev1[h] = g0.astype(BF16)
        pairs[h] = (g0 + g1).reshape(8, CHUNK, 128)

    copies[2].wait()
    states(head)
    gk[0].wait_recv()
    states(sib)
    step(gk, (3, 6))
    gq[0].start()
    states(down)
    states(up)
    states(far)
    gk[4].wait_recv()
    states(down_s)
    gk[5].wait_recv()
    states(up_s)
    gk[6].wait_recv()
    states(far_s)
    pl.semaphore_wait(in_sem.at[1], 2)

    a2a = [
        remote(send.at[z_at(d)], recv.at[z], as_sem.at[d], ar_sem.at[d], ctx_to=ctx_z(d))
        for d in range(1, Z)
    ]

    def chunk_state(j):
        p = [pairs[h, j] for h in range(8)]
        for i in range(4):
            lev2[i, j] = p[2 * i].astype(BF16)
        p4 = [p[2 * i] + p[2 * i + 1] for i in range(4)]
        lev3[0, j] = p4[0].astype(BF16)
        lev3[1, j] = p4[2].astype(BF16)
        low = p4[0] + p4[1]
        lev4[j] = low.astype(BF16)
        send[j] = (low + p4[2] + p4[3]).astype(BF16)

    for d in (4, 3, 5, 2, 6, 1, 7):
        chunk_state(z_at(d))
        a2a[d - 1].start()
    chunk_state(z)
    recv[z] = send[z]

    z_next = remote(send, zst.at[0], zs_sem.at[0, 0], zr_sem.at[0, 0], ctx_to=ctx_z(1))

    causal = lax.broadcasted_iota(jnp.int32, (GROUP, GROUP), 0) >= lax.broadcasted_iota(
        jnp.int32, (GROUP, GROUP), 1
    )
    heads = [slice(h * GROUP, (h + 1) * GROUP) for h in range(4)]

    def share(i, level, h):
        return sh[i, 16 * h + level : 16 * h + level + 1, :]

    def add_far(i, state, level):
        f = nt(state, qbuf[pl.ds(2 * i, 2)].reshape(256, 128))
        for h in range(4):
            total[i, heads[h], :] += f[heads[h]] * share(i, level, h)

    def near(i):
        for odd in range(2):
            g = 2 * i + odd
            cols = slice(odd * GROUP, (odd + 1) * GROUP)
            q = qbuf[g]
            s = jnp.where(causal, nt(q, kbuf[g]), 0.0).astype(BF16)
            f0 = nt(vt[i, :, cols], s)
            if odd:
                f1 = nt(lev1[i], q)
            for h in range(4):
                t = f0[heads[h]] * share(i, 0, h)[:, cols]
                if odd:
                    t += f1[heads[h]] * share(i, 1, h)[:, cols]
                total[i, heads[h], cols] = t

        @pl.when(i % 2 == 1)
        def _():
            add_far(i, lev2[i // 2].reshape(512, 128), 2)

        @pl.when(i // 2 % 2 == 1)
        def _():
            add_far(i, lev3[i // 4].reshape(512, 128), 3)

        @pl.when(i // 4 == 1)
        def _():
            add_far(i, lev4[...].reshape(512, 128), 4)

    copies[3].wait()
    near(head)

    @pl.when(z % 2 == 0)
    def _():
        z_next.start()

    step(gq, (1, 4), (2, 5))

    @pl.loop(0, 2)
    def _(e):
        near((y + 1 + 2 * e) % Y * 2 + c)

    step(gq, (3, 6))

    for cp in a2a:
        cp.wait_recv()
    r = [recv[i].astype(F32) for i in range(8)]
    s01, s23, s45, s67 = (r[2 * i] + r[2 * i + 1] for i in range(4))
    s03 = s01 + s23
    row = s03 + s45 + s67
    row_f[...] = row

    def x_copy(to):
        return remote(row_f, row_r.at[x], xs_sem.at[to], xr_sem.at[x], ctx_to=to * Z + z)

    for to, sender in ((3, x < 2), (1, x == 0)):

        @pl.when(sender)
        def _():
            x_copy(to).start()

    row_b[...] = row.astype(BF16)
    pair6[0] = s01.astype(BF16)
    pair6[1] = s45.astype(BF16)
    half7[...] = s03.astype(BF16)

    def t_copy(to):
        ctx_to = (x + 1) % X * Z + to
        return remote(row_b, xst.at[0, z], bs_sem.at[0, to], br_sem.at[0, z], ctx_to=ctx_to)

    def z_copy(level, to):
        src = (None, pair6.at[to // 4], half7)[level]
        return remote(
            src, zst.at[level, z], zs_sem.at[level, to], zr_sem.at[level, z], ctx_to=x * Z + to
        )

    def z_send(level, to):
        @pl.when(z != to)
        def _():
            z_copy(level, to).start()

    low_z, high_z = range(4), range(4, 8)
    even = x % 2 == 0

    @pl.when(even)
    def _():
        for to in low_z:
            t_copy(to).start()

    for to in (2, 3):
        z_send(1, to)

    @pl.when(even)
    def _():
        for to in high_z:
            t_copy(to).start()

    for to in high_z:
        z_send(2, to)
    for to in (6, 7):
        z_send(1, to)

    zst[1, z] = pair6[z // 4]
    zst[2, z] = half7[...]

    gq[0].wait_recv()
    near(far)
    near(sib)

    def b_copy(to):
        ctx_to = jnp.where(x == 1, 2, x) * Z + to
        return remote(both, xst.at[1, z], bs_sem.at[1, to], br_sem.at[1, z], ctx_to=ctx_to)

    def b_send(to):
        @pl.when(jnp.logical_or(x == 1, z != to))
        def _():
            b_copy(to).start()

    def landed(sems, dst, sources):
        for j in sources:

            @pl.when(z != j)
            def _():
                remote(half7, dst.at[j], sems.at[j], sems.at[j]).wait_recv()

    def x_wait(s):
        remote(row_f, row_r.at[s], xs_sem.at[s], xr_sem.at[s]).wait_recv()

    @pl.when(x == 1)
    def _():
        x_wait(0)
        both[...] = (row_r[0] + row_f[...]).astype(BF16)

    @pl.when(x == 3)
    def _():
        x_wait(0)
        x_wait(1)
        t = (row_r[0] + row_r[1]).astype(BF16)
        both[...] = t
        xst[1, z] = t

    @pl.when(x % 2 == 1)
    def _():
        for to in range(Z):
            b_send(to)

    @pl.when(x < 2)
    def _():
        xst[1] = jnp.zeros((8, CHUNK, 128), BF16)

    for i in (4, 5, 6):
        gq[i].wait_recv()

    @pl.loop(1, 4)
    def _(e):
        near((y + e) % Y * 2 + 1 - c)

    def add_all(state, level):
        @pl.loop(0, 4)
        def _(m):
            for i in range(2):
                add_far(2 * m + i, state.reshape(512, 128), level)

    @pl.when(z % 2 == 1)
    def _():
        z_next.wait_recv()
        add_all(zst[0], 5)

    for level in (1, 2):

        @pl.when((z >> level) % 2 == 1)
        def _():
            landed(zr_sem.at[level], zst.at[level], range(Z))
            add_all(zst[level], 5 + level)

    @pl.when(x % 2 == 1)
    def _():
        landed(br_sem.at[0], xst.at[0], range(Z))
        remote(half7, xst.at[0, z], br_sem.at[0, z], br_sem.at[0, z]).wait_recv()
        add_all(xst[0], 8)

    @pl.when(x >= 2)
    def _():
        landed(br_sem.at[1], xst.at[1], range(Z))

    @pl.when(x == 2)
    def _():
        remote(half7, xst.at[1, z], br_sem.at[1, z], br_sem.at[1, z]).wait_recv()

    for cp in gk + gq + a2a:
        cp.wait_send()

    @pl.when(z % 2 == 0)
    def _():
        z_next.wait_send()

    for to, sender in ((3, x < 2), (1, x == 0)):

        @pl.when(sender)
        def _():
            x_copy(to).wait_send()

    for level, targets in ((2, high_z), (1, (2, 3, 6, 7))):
        for to in targets:

            @pl.when(z != to)
            def _():
                z_copy(level, to).wait_send()

    @pl.when(even)
    def _():
        for to in range(Z):
            t_copy(to).wait_send()

    @pl.when(x % 2 == 1)
    def _():
        for to in range(Z):

            @pl.when(jnp.logical_or(x == 1, z != to))
            def _():
                b_copy(to).wait_send()


def finish(qbuf, sh, total, xst, out, obuf, o_sem):
    def o_copy(i):
        g = pl.ds(2 * i, 2)
        return pltpu.make_async_copy(obuf.at[g], out.at[g], o_sem.at[i])

    @pl.loop(0, 4)
    def _(m):
        for i in (2 * m, 2 * m + 1):
            f = nt(xst[1].reshape(512, 128), qbuf[pl.ds(2 * i, 2)].reshape(256, 128))
            for h in range(4):
                rows = slice(h * GROUP, (h + 1) * GROUP)
                lane = 16 * h + 9
                t = total[i, rows, :] + f[rows] * sh[i, lane : lane + 1, :]
                obuf[pl.ds(2 * i, 2), :, rows] = t.astype(BF16).T.reshape(2, GROUP, GROUP)
            o_copy(i).start()

    for i in range(8):
        o_copy(i).wait()


def local(queries, keys, values, tier_weight_rows, level_table):
    tokens, columns = values.shape
    groups = tokens // GROUP
    anywhere = pl.BlockSpec(memory_space=pl.ANY)
    vm = pltpu.VMEM
    kept = (
        vm((16, GROUP, 128), BF16),
        vm((8, 64, 256), F32),
        vm((8, 512, 256), F32),
        vm((2, 8, CHUNK, 128), BF16),
    )
    in_vmem = [pl.BlockSpec(memory_space=pltpu.VMEM)] * len(kept)
    parts = pl.pallas_call(
        kernel,
        out_shape=kept,
        in_specs=[pl.BlockSpec(memory_space=pltpu.MemorySpace.HBM)] * 5,
        out_specs=in_vmem,
        scratch_shapes=[
            vm((16, GROUP, 128), BF16),
            vm((16, GROUP, 512), BF16),
            vm((8, 512, 256), BF16),
            vm((10, 2048), jnp.int32),
            pltpu.SMEM((4, 16), F32),
            vm((8, 8, CHUNK, 128), F32),
            vm((8, 512, 128), BF16),
            vm((4, 8, CHUNK, 128), BF16),
            vm((2, 8, CHUNK, 128), BF16),
            vm((8, CHUNK, 128), BF16),
            vm((8, CHUNK, 128), BF16),
            vm((8, CHUNK, 128), BF16),
            vm((2, CHUNK, 128), BF16),
            vm((CHUNK, 128), BF16),
            vm((CHUNK, 128), F32),
            vm((CHUNK, 128), BF16),
            vm((2, CHUNK, 128), F32),
            vm((CHUNK, 128), BF16),
            vm((3, 8, CHUNK, 128), BF16),
            DMA((4,)),
            DMA((8,)),
            DMA((2, 7)),
            DMA((2, 7)),
            DMA((8,)),
            DMA((8,)),
            DMA((3, 8)),
            DMA((3, 8)),
            DMA((4,)),
            DMA((2,)),
            DMA((2, 8)),
            DMA((2, 8)),
            pltpu.SemaphoreType.REGULAR((2,)),
        ],
        compiler_params=pltpu.CompilerParams(
            collective_id=0, has_side_effects=True, vmem_limit_bytes=24 * 2**20
        ),
    )(*(
        pltpu.with_memory_space_constraint(arg, pltpu.MemorySpace.HBM)
        for arg in (
            queries.reshape(2, GROUP, 128),
            keys.reshape(2, GROUP, 128),
            values.reshape(groups, GROUP, columns),
            tier_weight_rows,
            level_table.T,
        )
    ))
    out = pl.pallas_call(
        finish,
        out_shape=jax.ShapeDtypeStruct((groups, GROUP, columns), BF16),
        in_specs=in_vmem,
        out_specs=anywhere,
        scratch_shapes=[vm((groups, GROUP, columns), BF16), DMA((8,))],
        compiler_params=pltpu.CompilerParams(vmem_limit_bytes=12 * 2**20),
    )(*parts)
    return out.reshape(tokens, columns)


def solution(mesh):
    return jax.shard_map(
        local,
        mesh=mesh,
        in_specs=(
            P(("ctx", "head"), None),
            P(("ctx", "head"), None),
            P("ctx", "head"),
            P(None, "ctx"),
            P(None, "head"),
        ),
        out_specs=P("ctx", "head"),
        check_vma=False,
    )
```

```python
import functools

import jax
import jax.numpy as jnp
from jax import lax
from jax.experimental import pallas as pl
from jax.experimental.pallas import tpu as pltpu
from jax.sharding import PartitionSpec as P

GROUP = 128
X, Y, Z = 4, 4, 8
CHUNK = 64
F32, BF16 = jnp.float32, jnp.bfloat16
DMA = pltpu.SemaphoreType.DMA


def nt(a, b):
    return lax.dot_general(a, b, (((1,), (1,)), ((), ())), preferred_element_type=F32)


def nn(a, b):
    return jnp.dot(a, b, preferred_element_type=F32)


def kernel(
    q_in, k_in, v_in, rows_in, table_in,
    qbuf, sh, total, xst,
    kbuf, vbuf, vt, rows, table, pairs, lev1, lev2, lev3, lev4,
    send, recv, pair6, half7, row_f, row_b, row_r, both, zst,
    loc_sem, v_sem, gs_sem, gr_sem, as_sem, ar_sem, zs_sem, zr_sem,
    xs_sem, xr_sem, bs_sem, br_sem, in_sem,
):
    ctx = lax.axis_index("ctx")
    head = lax.axis_index("head")
    x, z = ctx // Z, ctx % Z
    y, c = head // 2, head % 2
    sib = y * 2 + 1 - c
    up = ((y + 1) % Y) * 2 + c
    down = ((y + 3) % Y) * 2 + c
    far = ((y + 2) % Y) * 2 + c
    up_s, down_s, far_s = (((y + d) % Y) * 2 + 1 - c for d in (1, 3, 2))

    def remote(src, dst, ss, rs, ctx_to=ctx, head_to=head):
        return pltpu.make_async_remote_copy(
            src, dst, ss, rs, device_id=(ctx_to, head_to), device_id_type=pl.DeviceIdType.MESH
        )

    def z_at(d):
        return (z + d) % Z

    def ctx_z(d):
        return x * Z + z_at(d)

    copies = [
        pltpu.make_async_copy(rows_in, rows, loc_sem.at[0]),
        pltpu.make_async_copy(table_in, table, loc_sem.at[1]),
        pltpu.make_async_copy(k_in, kbuf.at[pl.ds(2 * head, 2)], loc_sem.at[2]),
        pltpu.make_async_copy(q_in, qbuf.at[pl.ds(2 * head, 2)], loc_sem.at[3]),
    ]
    v_copies = [
        pltpu.make_async_copy(v_in.at[pl.ds(2 * i, 2)], vbuf.at[pl.ds(2 * i, 2)], v_sem.at[i])
        for i in range(8)
    ]

    mesh_id = pl.DeviceIdType.MESH
    barrier = pltpu.get_barrier_semaphore()
    next_x = [((x + d) % X * Z + z, head) for d in (1, X - 1)]
    next_z = [(ctx_z(d), head) for d in (1, Z - 1)]
    partners = [(ctx, to) for to in (sib, up, down, far)] + next_z + next_x
    for to in partners:
        pl.semaphore_signal(barrier, 1, device_id=to, device_id_type=mesh_id)
    for cp in copies + v_copies:
        cp.start()
    pl.semaphore_wait(barrier, len(partners))

    def gather(src, buf, n):
        def g(i, a, b, to):
            return remote(a, b, gs_sem.at[n, i], gr_sem.at[n, i], head_to=to)

        def shard(h):
            return buf.at[pl.ds(2 * h, 2)]

        return [
            g(0, src, shard(head), sib),
            g(1, src, shard(head), up),
            g(2, src, shard(head), down),
            g(3, src, shard(head), far),
            g(4, shard(down), shard(down), sib),
            g(5, shard(up), shard(up), sib),
            g(6, shard(far), shard(far), sib),
        ]

    def step(copies, *pairs):
        for landed, started in pairs:
            copies[landed].wait_recv()
            copies[started].start()

    gk = gather(k_in, kbuf, 0)
    gq = gather(q_in, qbuf, 1)
    for i in (3, 1, 2, 0):
        gk[i].start()
    for to in next_z + next_x:
        pl.semaphore_signal(in_sem.at[0], 1, device_id=to, device_id_type=mesh_id)

    for cp in v_copies:
        cp.wait()

    @pl.loop(0, 8)
    def _(i):
        for odd in range(2):
            vt[i, :, odd * 128 : (odd + 1) * 128] = vbuf[2 * i + odd].T

    copies[0].wait()
    copies[1].wait()

    @pl.loop(0, 8)
    def _(i):
        r = rows[:, pl.ds(pl.multiple_of(i * 256, 256), 256)]
        ws = [jnp.zeros(r.shape, F32) for _ in range(4)]
        for cl in range(16):
            hit = r == cl
            ws = [jnp.where(hit, table[h, cl], w) for h, w in enumerate(ws)]
        for h, w in enumerate(ws):
            sh[i, pl.ds(16 * h, 10), :] = w / jnp.sum(w, axis=0, keepdims=True)

    pl.semaphore_wait(in_sem.at[0], 4)
    for d in (2, Z - 2):
        pl.semaphore_signal(
            in_sem.at[1], 1, device_id=(ctx_z(d), head), device_id_type=mesh_id
        )

    step(gk, (1, 4), (2, 5))
    for i in (3, 1, 2):
        gq[i].start()


    def states(h):
        g0 = nn(vt[h, :, :128], kbuf[2 * h])
        g1 = nn(vt[h, :, 128:], kbuf[2 * h + 1])
        lev1[h] = g0.astype(BF16)
        pairs[h] = (g0 + g1).reshape(8, CHUNK, 128)

    copies[2].wait()
    states(head)
    gk[0].wait_recv()
    states(sib)
    step(gk, (3, 6))
    gq[0].start()
    states(down)
    states(up)
    states(far)
    gk[4].wait_recv()
    states(down_s)
    gk[5].wait_recv()
    states(up_s)
    gk[6].wait_recv()
    states(far_s)
    pl.semaphore_wait(in_sem.at[1], 2)

    a2a = [
        remote(send.at[z_at(d)], recv.at[z], as_sem.at[d], ar_sem.at[d], ctx_to=ctx_z(d))
        for d in range(1, Z)
    ]

    def chunk_state(j):
        p = [pairs[h, j] for h in range(8)]
        for i in range(4):
            lev2[i, j] = p[2 * i].astype(BF16)
        p4 = [p[2 * i] + p[2 * i + 1] for i in range(4)]
        lev3[0, j] = p4[0].astype(BF16)
        lev3[1, j] = p4[2].astype(BF16)
        low = p4[0] + p4[1]
        lev4[j] = low.astype(BF16)
        send[j] = (low + p4[2] + p4[3]).astype(BF16)

    for d in (4, 3, 5, 2, 6, 1, 7):
        chunk_state(z_at(d))
        a2a[d - 1].start()
    chunk_state(z)
    recv[z] = send[z]

    z_next = remote(send, zst.at[0], zs_sem.at[0, 0], zr_sem.at[0, 0], ctx_to=ctx_z(1))

    causal = lax.broadcasted_iota(jnp.int32, (GROUP, GROUP), 0) >= lax.broadcasted_iota(
        jnp.int32, (GROUP, GROUP), 1
    )
    heads = [slice(h * GROUP, (h + 1) * GROUP) for h in range(4)]

    def share(i, level, h):
        return sh[i, 16 * h + level : 16 * h + level + 1, :]

    def add_far(i, state, level):
        f = nt(state, qbuf[pl.ds(2 * i, 2)].reshape(256, 128))
        for h in range(4):
            total[i, heads[h], :] += f[heads[h]] * share(i, level, h)

    def near(i):
        for odd in range(2):
            g = 2 * i + odd
            cols = slice(odd * GROUP, (odd + 1) * GROUP)
            q = qbuf[g]
            s = jnp.where(causal, nt(q, kbuf[g]), 0.0).astype(BF16)
            f0 = nt(vt[i, :, cols], s)
            if odd:
                f1 = nt(lev1[i], q)
            for h in range(4):
                t = f0[heads[h]] * share(i, 0, h)[:, cols]
                if odd:
                    t += f1[heads[h]] * share(i, 1, h)[:, cols]
                total[i, heads[h], cols] = t

        @pl.when(i % 2 == 1)
        def _():
            add_far(i, lev2[i // 2].reshape(512, 128), 2)

        @pl.when(i // 2 % 2 == 1)
        def _():
            add_far(i, lev3[i // 4].reshape(512, 128), 3)

        @pl.when(i // 4 == 1)
        def _():
            add_far(i, lev4[...].reshape(512, 128), 4)

    copies[3].wait()
    near(head)

    @pl.when(z % 2 == 0)
    def _():
        z_next.start()

    step(gq, (1, 4), (2, 5))

    @pl.loop(0, 2)
    def _(e):
        near((y + 1 + 2 * e) % Y * 2 + c)

    step(gq, (3, 6))

    for cp in a2a:
        cp.wait_recv()
    r = [recv[i].astype(F32) for i in range(8)]
    s01, s23, s45, s67 = (r[2 * i] + r[2 * i + 1] for i in range(4))
    s03 = s01 + s23
    row = s03 + s45 + s67
    row_f[...] = row

    def x_copy(to):
        return remote(row_f, row_r.at[x], xs_sem.at[to], xr_sem.at[x], ctx_to=to * Z + z)

    for to, sender in ((3, x < 2), (1, x == 0)):

        @pl.when(sender)
        def _():
            x_copy(to).start()

    row_b[...] = row.astype(BF16)
    pair6[0] = s01.astype(BF16)
    pair6[1] = s45.astype(BF16)
    half7[...] = s03.astype(BF16)

    def t_copy(to):
        ctx_to = (x + 1) % X * Z + to
        return remote(row_b, xst.at[0, z], bs_sem.at[0, to], br_sem.at[0, z], ctx_to=ctx_to)

    def z_copy(level, to):
        src = (None, pair6.at[to // 4], half7)[level]
        return remote(
            src, zst.at[level, z], zs_sem.at[level, to], zr_sem.at[level, z], ctx_to=x * Z + to
        )

    def z_send(level, to):
        @pl.when(z != to)
        def _():
            z_copy(level, to).start()

    high_z = range(4, 8)
    even = x % 2 == 0

    def t_send(*targets):
        @pl.when(even)
        def _():
            for to in targets:
                t_copy(to).start()

    t_send(0, 1)
    z_send(1, 2)
    z_send(1, 3)
    t_send(2, 3)
    z_send(2, 4)
    z_send(2, 5)
    t_send(4, 5)
    for to in (6, 7):
        z_send(2, to)
        z_send(1, to)
    t_send(6, 7)

    zst[1, z] = pair6[z // 4]
    zst[2, z] = half7[...]

    gq[0].wait_recv()
    near(far)
    near(sib)
    gq[4].wait_recv()
    gq[5].wait_recv()

    @pl.loop(0, 2)
    def _(e):
        near((y + 1 + 2 * e) % Y * 2 + 1 - c)

    def b_copy(to):
        ctx_to = jnp.where(x == 1, 2, x) * Z + to
        return remote(both, xst.at[1, z], bs_sem.at[1, to], br_sem.at[1, z], ctx_to=ctx_to)

    def b_send(to):
        @pl.when(jnp.logical_or(x == 1, z != to))
        def _():
            b_copy(to).start()

    def landed(sems, dst, sources):
        for j in sources:

            @pl.when(z != j)
            def _():
                remote(half7, dst.at[j], sems.at[j], sems.at[j]).wait_recv()

    def x_wait(s):
        remote(row_f, row_r.at[s], xs_sem.at[s], xr_sem.at[s]).wait_recv()

    @pl.when(x == 1)
    def _():
        x_wait(0)
        both[...] = (row_r[0] + row_f[...]).astype(BF16)

    @pl.when(x == 3)
    def _():
        x_wait(0)
        x_wait(1)
        t = (row_r[0] + row_r[1]).astype(BF16)
        both[...] = t
        xst[1, z] = t

    @pl.when(x % 2 == 1)
    def _():
        for to in range(Z):
            b_send(to)

    gq[6].wait_recv()
    near(far_s)

    def add_all(state, level):
        @pl.loop(0, 4)
        def _(m):
            for i in range(2):
                add_far(2 * m + i, state.reshape(512, 128), level)

    @pl.when(z % 2 == 1)
    def _():
        z_next.wait_recv()
        add_all(zst[0], 5)

    for level in (1, 2):

        @pl.when((z >> level) % 2 == 1)
        def _():
            landed(zr_sem.at[level], zst.at[level], range(Z))
            add_all(zst[level], 5 + level)

    @pl.when(x % 2 == 1)
    def _():
        landed(br_sem.at[0], xst.at[0], range(Z))
        remote(half7, xst.at[0, z], br_sem.at[0, z], br_sem.at[0, z]).wait_recv()

    @pl.when(x == 3)
    def _():
        add_all(xst[0], 8)

    @pl.when(x >= 2)
    def _():
        landed(br_sem.at[1], xst.at[1], range(Z))

    @pl.when(x == 2)
    def _():
        remote(half7, xst.at[1, z], br_sem.at[1, z], br_sem.at[1, z]).wait_recv()

    for cp in gk + gq + a2a:
        cp.wait_send()

    @pl.when(z % 2 == 0)
    def _():
        z_next.wait_send()

    for to, sender in ((3, x < 2), (1, x == 0)):

        @pl.when(sender)
        def _():
            x_copy(to).wait_send()

    for level, targets in ((2, high_z), (1, (2, 3, 6, 7))):
        for to in targets:

            @pl.when(z != to)
            def _():
                z_copy(level, to).wait_send()

    @pl.when(even)
    def _():
        for to in range(Z):
            t_copy(to).wait_send()

    @pl.when(x % 2 == 1)
    def _():
        for to in range(Z):

            @pl.when(jnp.logical_or(x == 1, z != to))
            def _():
                b_copy(to).wait_send()


def finish(qbuf, sh, total, xst, out, obuf, o_sem):
    def o_copy(i):
        g = pl.ds(2 * i, 2)
        return pltpu.make_async_copy(obuf.at[g], out.at[g], o_sem.at[i])

    def run(level):
        @pl.loop(0, 4)
        def _(m):
            for i in (2 * m, 2 * m + 1):
                if level:
                    state = xst[level - 8].reshape(512, 128)
                    f = nt(state, qbuf[pl.ds(2 * i, 2)].reshape(256, 128))
                for h in range(4):
                    rows = slice(h * GROUP, (h + 1) * GROUP)
                    t = total[i, rows, :]
                    if level:
                        lane = 16 * h + level
                        t += f[rows] * sh[i, lane : lane + 1, :]
                    obuf[pl.ds(2 * i, 2), :, rows] = t.astype(BF16).T.reshape(2, GROUP, GROUP)
                o_copy(i).start()

    x = lax.axis_index("ctx") // Z
    pl.when(x >= 2)(lambda: run(9))
    pl.when(x == 1)(lambda: run(8))
    pl.when(x == 0)(lambda: run(None))

    for i in range(8):
        o_copy(i).wait()


def local(queries, keys, values, tier_weight_rows, level_table):
    tokens, columns = values.shape
    groups = tokens // GROUP
    anywhere = pl.BlockSpec(memory_space=pl.ANY)
    vm = pltpu.VMEM
    kept = (
        vm((16, GROUP, 128), BF16),
        vm((8, 64, 256), F32),
        vm((8, 512, 256), F32),
        vm((2, 8, CHUNK, 128), BF16),
    )
    in_vmem = [pl.BlockSpec(memory_space=pltpu.VMEM)] * len(kept)
    parts = pl.pallas_call(
        kernel,
        out_shape=kept,
        in_specs=[pl.BlockSpec(memory_space=pltpu.MemorySpace.HBM)] * 5,
        out_specs=in_vmem,
        scratch_shapes=[
            vm((16, GROUP, 128), BF16),
            vm((16, GROUP, 512), BF16),
            vm((8, 512, 256), BF16),
            vm((10, 2048), jnp.int32),
            pltpu.SMEM((4, 16), F32),
            vm((8, 8, CHUNK, 128), F32),
            vm((8, 512, 128), BF16),
            vm((4, 8, CHUNK, 128), BF16),
            vm((2, 8, CHUNK, 128), BF16),
            vm((8, CHUNK, 128), BF16),
            vm((8, CHUNK, 128), BF16),
            vm((8, CHUNK, 128), BF16),
            vm((2, CHUNK, 128), BF16),
            vm((CHUNK, 128), BF16),
            vm((CHUNK, 128), F32),
            vm((CHUNK, 128), BF16),
            vm((2, CHUNK, 128), F32),
            vm((CHUNK, 128), BF16),
            vm((3, 8, CHUNK, 128), BF16),
            DMA((4,)),
            DMA((8,)),
            DMA((2, 7)),
            DMA((2, 7)),
            DMA((8,)),
            DMA((8,)),
            DMA((3, 8)),
            DMA((3, 8)),
            DMA((4,)),
            DMA((2,)),
            DMA((2, 8)),
            DMA((2, 8)),
            pltpu.SemaphoreType.REGULAR((2,)),
        ],
        compiler_params=pltpu.CompilerParams(
            collective_id=0, has_side_effects=True, vmem_limit_bytes=24 * 2**20
        ),
    )(*(
        pltpu.with_memory_space_constraint(arg, pltpu.MemorySpace.HBM)
        for arg in (
            queries.reshape(2, GROUP, 128),
            keys.reshape(2, GROUP, 128),
            values.reshape(groups, GROUP, columns),
            tier_weight_rows,
            level_table.T,
        )
    ))
    out = pl.pallas_call(
        finish,
        out_shape=jax.ShapeDtypeStruct((groups, GROUP, columns), BF16),
        in_specs=in_vmem,
        out_specs=anywhere,
        scratch_shapes=[vm((groups, GROUP, columns), BF16), DMA((8,))],
        compiler_params=pltpu.CompilerParams(vmem_limit_bytes=12 * 2**20),
    )(*parts)
    return out.reshape(tokens, columns)


def solution(mesh):
    return jax.shard_map(
        local,
        mesh=mesh,
        in_specs=(
            P(("ctx", "head"), None),
            P(("ctx", "head"), None),
            P("ctx", "head"),
            P(None, "ctx"),
            P(None, "head"),
        ),
        out_specs=P("ctx", "head"),
        check_vma=False,
    )
```

```python
import functools

import jax
import jax.numpy as jnp
from jax import lax
from jax.experimental import pallas as pl
from jax.experimental.pallas import tpu as pltpu
from jax.sharding import PartitionSpec as P

GROUP = 128
X, Y, Z = 4, 4, 8
CHUNK = 64
F32, BF16 = jnp.float32, jnp.bfloat16
DMA = pltpu.SemaphoreType.DMA


def nt(a, b):
    return lax.dot_general(a, b, (((1,), (1,)), ((), ())), preferred_element_type=F32)


def nn(a, b):
    return jnp.dot(a, b, preferred_element_type=F32)


def kernel(
    q_in, k_in, v_in, rows_in, table_in,
    qbuf, sh, total, xst,
    kbuf, vbuf, vt, rows, table, pairs, lev1, lev2, lev3, lev4,
    send, recv, pair6, half7, row_f, row_b, row_r, both, zst,
    loc_sem, v_sem, gs_sem, gr_sem, as_sem, ar_sem, zs_sem, zr_sem,
    xs_sem, xr_sem, bs_sem, br_sem, ps_sem, in_sem,
):
    ctx = lax.axis_index("ctx")
    head = lax.axis_index("head")
    x, z = ctx // Z, ctx % Z
    y, c = head // 2, head % 2
    sib = y * 2 + 1 - c
    up = ((y + 1) % Y) * 2 + c
    down = ((y + 3) % Y) * 2 + c
    far = ((y + 2) % Y) * 2 + c
    up_s, down_s, far_s = (((y + d) % Y) * 2 + 1 - c for d in (1, 3, 2))

    def remote(src, dst, ss, rs, ctx_to=ctx, head_to=head):
        return pltpu.make_async_remote_copy(
            src, dst, ss, rs, device_id=(ctx_to, head_to), device_id_type=pl.DeviceIdType.MESH
        )

    def z_at(d):
        return (z + d) % Z

    def ctx_z(d):
        return x * Z + z_at(d)

    copies = [
        pltpu.make_async_copy(rows_in, rows, loc_sem.at[0]),
        pltpu.make_async_copy(table_in, table, loc_sem.at[1]),
        pltpu.make_async_copy(k_in, kbuf.at[pl.ds(2 * head, 2)], loc_sem.at[2]),
        pltpu.make_async_copy(q_in, qbuf.at[pl.ds(2 * head, 2)], loc_sem.at[3]),
    ]
    v_copies = [
        pltpu.make_async_copy(v_in.at[pl.ds(2 * i, 2)], vbuf.at[pl.ds(2 * i, 2)], v_sem.at[i])
        for i in range(8)
    ]

    mesh_id = pl.DeviceIdType.MESH
    barrier = pltpu.get_barrier_semaphore()
    next_x = [((x + d) % X * Z + z, head) for d in (1, X - 1)]
    next_z = [(ctx_z(d), head) for d in (1, Z - 1)]
    partners = [(ctx, to) for to in (sib, up, down, far)] + next_z + next_x
    for to in partners:
        pl.semaphore_signal(barrier, 1, device_id=to, device_id_type=mesh_id)
    for cp in copies + v_copies:
        cp.start()
    pl.semaphore_wait(barrier, len(partners))

    def gather(src, buf, n):
        def g(i, a, b, to):
            return remote(a, b, gs_sem.at[n, i], gr_sem.at[n, i], head_to=to)

        def shard(h):
            return buf.at[pl.ds(2 * h, 2)]

        return [
            g(0, src, shard(head), sib),
            g(1, src, shard(head), up),
            g(2, src, shard(head), down),
            g(3, src, shard(head), far),
            g(4, shard(down), shard(down), sib),
            g(5, shard(up), shard(up), sib),
            g(6, shard(far), shard(far), sib),
        ]

    def step(copies, *pairs):
        for landed, started in pairs:
            copies[landed].wait_recv()
            copies[started].start()

    gk = gather(k_in, kbuf, 0)
    gq = gather(q_in, qbuf, 1)
    for i in (3, 1, 2, 0):
        gk[i].start()
    for to in next_z + next_x:
        pl.semaphore_signal(in_sem.at[0], 1, device_id=to, device_id_type=mesh_id)

    for cp in v_copies:
        cp.wait()

    @pl.loop(0, 8)
    def _(i):
        for odd in range(2):
            vt[i, :, odd * 128 : (odd + 1) * 128] = vbuf[2 * i + odd].T

    copies[0].wait()
    copies[1].wait()

    @pl.loop(0, 8)
    def _(i):
        r = rows[:, pl.ds(pl.multiple_of(i * 256, 256), 256)]
        ws = [jnp.zeros(r.shape, F32) for _ in range(4)]
        for cl in range(16):
            hit = r == cl
            ws = [jnp.where(hit, table[h, cl], w) for h, w in enumerate(ws)]
        for h, w in enumerate(ws):
            sh[i, pl.ds(16 * h, 10), :] = w / jnp.sum(w, axis=0, keepdims=True)

    pl.semaphore_wait(in_sem.at[0], 4)
    for d in (2, Z - 2):
        pl.semaphore_signal(
            in_sem.at[1], 1, device_id=(ctx_z(d), head), device_id_type=mesh_id
        )

    step(gk, (1, 4), (2, 5))
    for i in (3, 1, 2):
        gq[i].start()


    def states(h):
        g0 = nn(vt[h, :, :128], kbuf[2 * h])
        g1 = nn(vt[h, :, 128:], kbuf[2 * h + 1])
        lev1[h] = g0.astype(BF16)
        pairs[h] = (g0 + g1).reshape(8, CHUNK, 128)

    copies[2].wait()
    states(head)
    gk[0].wait_recv()
    states(sib)
    step(gk, (3, 6))
    gq[0].start()
    states(down)
    states(up)
    states(far)
    gk[4].wait_recv()
    states(down_s)
    gk[5].wait_recv()
    states(up_s)
    gk[6].wait_recv()
    states(far_s)
    pl.semaphore_wait(in_sem.at[1], 2)

    a2a = [
        remote(send.at[z_at(d)], recv.at[z], as_sem.at[d], ar_sem.at[d], ctx_to=ctx_z(d))
        for d in range(1, Z)
    ]

    def chunk_state(j):
        p = [pairs[h, j] for h in range(8)]
        for i in range(4):
            lev2[i, j] = p[2 * i].astype(BF16)
        p4 = [p[2 * i] + p[2 * i + 1] for i in range(4)]
        lev3[0, j] = p4[0].astype(BF16)
        lev3[1, j] = p4[2].astype(BF16)
        low = p4[0] + p4[1]
        lev4[j] = low.astype(BF16)
        send[j] = (low + p4[2] + p4[3]).astype(BF16)

    for d in (4, 3, 5, 2, 6, 1, 7):
        chunk_state(z_at(d))
        a2a[d - 1].start()
    chunk_state(z)
    recv[z] = send[z]

    z_next = remote(send, zst.at[0], zs_sem.at[0, 0], zr_sem.at[0, 0], ctx_to=ctx_z(1))

    @pl.when(z % 2 == 0)
    def _():
        z_next.start()

    causal = lax.broadcasted_iota(jnp.int32, (GROUP, GROUP), 0) >= lax.broadcasted_iota(
        jnp.int32, (GROUP, GROUP), 1
    )
    heads = [slice(h * GROUP, (h + 1) * GROUP) for h in range(4)]

    def share(i, level, h):
        return sh[i, 16 * h + level : 16 * h + level + 1, :]

    def add_far(i, state, level):
        f = nt(state, qbuf[pl.ds(2 * i, 2)].reshape(256, 128))
        for h in range(4):
            total[i, heads[h], :] += f[heads[h]] * share(i, level, h)

    def near(i):
        for odd in range(2):
            g = 2 * i + odd
            cols = slice(odd * GROUP, (odd + 1) * GROUP)
            q = qbuf[g]
            s = jnp.where(causal, nt(q, kbuf[g]), 0.0).astype(BF16)
            f0 = nt(vt[i, :, cols], s)
            if odd:
                f1 = nt(lev1[i], q)
            for h in range(4):
                t = f0[heads[h]] * share(i, 0, h)[:, cols]
                if odd:
                    t += f1[heads[h]] * share(i, 1, h)[:, cols]
                total[i, heads[h], cols] = t

        @pl.when(i % 2 == 1)
        def _():
            add_far(i, lev2[i // 2].reshape(512, 128), 2)

        @pl.when(i // 2 % 2 == 1)
        def _():
            add_far(i, lev3[i // 4].reshape(512, 128), 3)

        @pl.when(i // 4 == 1)
        def _():
            add_far(i, lev4[...].reshape(512, 128), 4)

    copies[3].wait()
    near(head)

    step(gq, (1, 4), (2, 5))

    @pl.loop(0, 2)
    def _(e):
        near((y + 1 + 2 * e) % Y * 2 + c)

    step(gq, (3, 6))

    for cp in a2a:
        cp.wait_recv()
    r = [recv[i].astype(F32) for i in range(8)]
    s01, s23, s45, s67 = (r[2 * i] + r[2 * i + 1] for i in range(4))
    s03 = s01 + s23
    row = s03 + s45 + s67
    row_f[...] = row

    def x_copy(to):
        return remote(row_f, row_r.at[x], xs_sem.at[to], xr_sem.at[x], ctx_to=to * Z + z)

    for to, sender in ((3, x < 2), (1, x == 0)):

        @pl.when(sender)
        def _():
            x_copy(to).start()

    row_b[...] = row.astype(BF16)
    pair6[0] = s01.astype(BF16)
    pair6[1] = s45.astype(BF16)
    half7[...] = s03.astype(BF16)

    def t_copy(to):
        ctx_to = (x + 1) % X * Z + to
        return remote(row_b, xst.at[0, z], bs_sem.at[0, to], br_sem.at[0, z], ctx_to=ctx_to)

    def z_copy(level, to):
        src = (None, pair6.at[to // 4], half7)[level]
        return remote(
            src, zst.at[level, z], zs_sem.at[level, to], zr_sem.at[level, z], ctx_to=x * Z + to
        )

    def direct(level, to):
        ok = z != to
        if level == 2:
            ok = jnp.logical_and(ok, z >= 4)
        return ok

    def z_send(level, to):
        @pl.when(direct(level, to))
        def _():
            z_copy(level, to).start()

    mate = jnp.maximum(z - 4, 0)

    def pass_on(to):
        slot = zst.at[2, mate]
        return remote(slot, slot, ps_sem.at[to - 4], zr_sem.at[2, mate], ctx_to=x * Z + to)

    high_z = range(4, 8)
    even = x % 2 == 0

    def t_send(*targets):
        @pl.when(even)
        def _():
            for to in targets:
                t_copy(to).start()

    @pl.when(z < 4)
    def _():
        z_copy(2, z + 4).start()

    t_send(0, 1)
    z_send(1, 2)
    z_send(1, 3)
    t_send(2, 3)
    z_send(2, 4)
    z_send(2, 5)
    t_send(4, 5)
    for to in (6, 7):
        z_send(2, to)
        z_send(1, to)
    t_send(6, 7)

    zst[1, z] = pair6[z // 4]
    zst[2, z] = half7[...]

    gq[0].wait_recv()
    near(far)
    near(sib)
    gq[4].wait_recv()
    near(down_s)

    def b_copy(to):
        ctx_to = jnp.where(x == 1, 2, x) * Z + to
        return remote(both, xst.at[1, z], bs_sem.at[1, to], br_sem.at[1, z], ctx_to=ctx_to)

    def b_send(to):
        @pl.when(jnp.logical_or(x == 1, z != to))
        def _():
            b_copy(to).start()

    def landed(sems, dst, sources, had=None):
        for j in sources:
            there = z == j
            if had is not None:
                there = jnp.logical_or(there, had == j)

            @pl.when(jnp.logical_not(there))
            def _():
                remote(half7, dst.at[j], sems.at[j], sems.at[j]).wait_recv()

    def x_wait(s):
        remote(row_f, row_r.at[s], xs_sem.at[s], xr_sem.at[s]).wait_recv()

    @pl.when(x == 1)
    def _():
        x_wait(0)
        both[...] = (row_r[0] + row_f[...]).astype(BF16)

    @pl.when(x == 3)
    def _():
        x_wait(0)
        x_wait(1)
        t = (row_r[0] + row_r[1]).astype(BF16)
        both[...] = t
        xst[1, z] = t

    @pl.when(x % 2 == 1)
    def _():
        for to in range(Z):
            b_send(to)

    gq[5].wait_recv()
    gq[6].wait_recv()

    @pl.loop(1, 3)
    def _(e):
        near((y + e) % Y * 2 + 1 - c)

    @pl.when(z >= 4)
    def _():
        remote(half7, zst.at[2, mate], zr_sem.at[2, mate], zr_sem.at[2, mate]).wait_recv()
        for to in high_z:

            @pl.when(z != to)
            def _():
                pass_on(to).start()

    def add_all(state, level):
        @pl.loop(0, 4)
        def _(m):
            for i in range(2):
                add_far(2 * m + i, state.reshape(512, 128), level)

    @pl.when(z % 2 == 1)
    def _():
        z_next.wait_recv()
        add_all(zst[0], 5)

    for level in (1, 2):

        @pl.when((z >> level) % 2 == 1)
        def _():
            landed(zr_sem.at[level], zst.at[level], range(Z), mate if level == 2 else None)
            add_all(zst[level], 5 + level)

    @pl.when(x % 2 == 1)
    def _():
        landed(br_sem.at[0], xst.at[0], range(Z))
        remote(half7, xst.at[0, z], br_sem.at[0, z], br_sem.at[0, z]).wait_recv()

    @pl.when(x == 3)
    def _():
        add_all(xst[0], 8)

    @pl.when(x >= 2)
    def _():
        landed(br_sem.at[1], xst.at[1], range(Z))

    @pl.when(x == 2)
    def _():
        remote(half7, xst.at[1, z], br_sem.at[1, z], br_sem.at[1, z]).wait_recv()

    for cp in gk + gq + a2a:
        cp.wait_send()

    @pl.when(z % 2 == 0)
    def _():
        z_next.wait_send()

    for to, sender in ((3, x < 2), (1, x == 0)):

        @pl.when(sender)
        def _():
            x_copy(to).wait_send()

    for level, targets in ((2, high_z), (1, (2, 3, 6, 7))):
        for to in targets:

            @pl.when(direct(level, to))
            def _():
                z_copy(level, to).wait_send()

    @pl.when(z < 4)
    def _():
        z_copy(2, z + 4).wait_send()

    @pl.when(z >= 4)
    def _():
        for to in high_z:

            @pl.when(z != to)
            def _():
                pass_on(to).wait_send()

    @pl.when(even)
    def _():
        for to in range(Z):
            t_copy(to).wait_send()

    @pl.when(x % 2 == 1)
    def _():
        for to in range(Z):

            @pl.when(jnp.logical_or(x == 1, z != to))
            def _():
                b_copy(to).wait_send()


def finish(qbuf, sh, total, xst, out, obuf, o_sem):
    def o_copy(i):
        g = pl.ds(2 * i, 2)
        return pltpu.make_async_copy(obuf.at[g], out.at[g], o_sem.at[i])

    def run(level):
        @pl.loop(0, 4)
        def _(m):
            for i in (2 * m, 2 * m + 1):
                if level:
                    state = xst[level - 8].reshape(512, 128)
                    f = nt(state, qbuf[pl.ds(2 * i, 2)].reshape(256, 128))
                for h in range(4):
                    rows = slice(h * GROUP, (h + 1) * GROUP)
                    t = total[i, rows, :]
                    if level:
                        lane = 16 * h + level
                        t += f[rows] * sh[i, lane : lane + 1, :]
                    obuf[pl.ds(2 * i, 2), :, rows] = t.astype(BF16).T.reshape(2, GROUP, GROUP)
                o_copy(i).start()

    x = lax.axis_index("ctx") // Z
    pl.when(x >= 2)(lambda: run(9))
    pl.when(x == 1)(lambda: run(8))
    pl.when(x == 0)(lambda: run(None))

    for i in range(8):
        o_copy(i).wait()


def local(queries, keys, values, tier_weight_rows, level_table):
    tokens, columns = values.shape
    groups = tokens // GROUP
    anywhere = pl.BlockSpec(memory_space=pl.ANY)
    vm = pltpu.VMEM
    kept = (
        vm((16, GROUP, 128), BF16),
        vm((8, 64, 256), F32),
        vm((8, 512, 256), F32),
        vm((2, 8, CHUNK, 128), BF16),
    )
    in_vmem = [pl.BlockSpec(memory_space=pltpu.VMEM)] * len(kept)
    parts = pl.pallas_call(
        kernel,
        out_shape=kept,
        in_specs=[pl.BlockSpec(memory_space=pltpu.MemorySpace.HBM)] * 5,
        out_specs=in_vmem,
        scratch_shapes=[
            vm((16, GROUP, 128), BF16),
            vm((16, GROUP, 512), BF16),
            vm((8, 512, 256), BF16),
            vm((10, 2048), jnp.int32),
            pltpu.SMEM((4, 16), F32),
            vm((8, 8, CHUNK, 128), F32),
            vm((8, 512, 128), BF16),
            vm((4, 8, CHUNK, 128), BF16),
            vm((2, 8, CHUNK, 128), BF16),
            vm((8, CHUNK, 128), BF16),
            vm((8, CHUNK, 128), BF16),
            vm((8, CHUNK, 128), BF16),
            vm((2, CHUNK, 128), BF16),
            vm((CHUNK, 128), BF16),
            vm((CHUNK, 128), F32),
            vm((CHUNK, 128), BF16),
            vm((2, CHUNK, 128), F32),
            vm((CHUNK, 128), BF16),
            vm((3, 8, CHUNK, 128), BF16),
            DMA((4,)),
            DMA((8,)),
            DMA((2, 7)),
            DMA((2, 7)),
            DMA((8,)),
            DMA((8,)),
            DMA((3, 8)),
            DMA((3, 8)),
            DMA((4,)),
            DMA((2,)),
            DMA((2, 8)),
            DMA((2, 8)),
            DMA((4,)),
            pltpu.SemaphoreType.REGULAR((2,)),
        ],
        compiler_params=pltpu.CompilerParams(
            collective_id=0, has_side_effects=True, vmem_limit_bytes=24 * 2**20
        ),
    )(*(
        pltpu.with_memory_space_constraint(arg, pltpu.MemorySpace.HBM)
        for arg in (
            queries.reshape(2, GROUP, 128),
            keys.reshape(2, GROUP, 128),
            values.reshape(groups, GROUP, columns),
            tier_weight_rows,
            level_table.T,
        )
    ))
    out = pl.pallas_call(
        finish,
        out_shape=jax.ShapeDtypeStruct((groups, GROUP, columns), BF16),
        in_specs=in_vmem,
        out_specs=anywhere,
        scratch_shapes=[vm((groups, GROUP, columns), BF16), DMA((8,))],
        compiler_params=pltpu.CompilerParams(vmem_limit_bytes=12 * 2**20),
    )(*parts)
    return out.reshape(tokens, columns)


def solution(mesh):
    return jax.shard_map(
        local,
        mesh=mesh,
        in_specs=(
            P(("ctx", "head"), None),
            P(("ctx", "head"), None),
            P("ctx", "head"),
            P(None, "ctx"),
            P(None, "head"),
        ),
        out_specs=P("ctx", "head"),
        check_vma=False,
    )
```

```python
import functools

import jax
import jax.numpy as jnp
from jax import lax
from jax.experimental import pallas as pl
from jax.experimental.pallas import tpu as pltpu
from jax.sharding import PartitionSpec as P

GROUP = 128
X, Y, Z = 4, 4, 8
CHUNK = 64
F32, BF16 = jnp.float32, jnp.bfloat16
DMA = pltpu.SemaphoreType.DMA


def nt(a, b):
    return lax.dot_general(a, b, (((1,), (1,)), ((), ())), preferred_element_type=F32)


def nn(a, b):
    return jnp.dot(a, b, preferred_element_type=F32)


def kernel(
    q_in, k_in, v_in, rows_in, table_in,
    qbuf, sh, total, xst,
    kbuf, vbuf, vt, rows, table, pairs, lev1, lev2, lev3, lev4,
    send, recv, pair6, half7, row_f, row_b, row_r, both, zst,
    loc_sem, v_sem, gs_sem, gr_sem, as_sem, ar_sem, zs_sem, zr_sem,
    xs_sem, xr_sem, bs_sem, br_sem, ps_sem, in_sem,
):
    ctx = lax.axis_index("ctx")
    head = lax.axis_index("head")
    x, z = ctx // Z, ctx % Z
    y, c = head // 2, head % 2
    sib = y * 2 + 1 - c
    up = ((y + 1) % Y) * 2 + c
    down = ((y + 3) % Y) * 2 + c
    far = ((y + 2) % Y) * 2 + c
    up_s, down_s, far_s = (((y + d) % Y) * 2 + 1 - c for d in (1, 3, 2))

    def remote(src, dst, ss, rs, ctx_to=ctx, head_to=head):
        return pltpu.make_async_remote_copy(
            src, dst, ss, rs, device_id=(ctx_to, head_to), device_id_type=pl.DeviceIdType.MESH
        )

    def z_at(d):
        return (z + d) % Z

    def ctx_z(d):
        return x * Z + z_at(d)

    copies = [
        pltpu.make_async_copy(rows_in, rows, loc_sem.at[0]),
        pltpu.make_async_copy(table_in, table, loc_sem.at[1]),
        pltpu.make_async_copy(k_in, kbuf.at[pl.ds(2 * head, 2)], loc_sem.at[2]),
        pltpu.make_async_copy(q_in, qbuf.at[pl.ds(2 * head, 2)], loc_sem.at[3]),
    ]
    v_copies = [
        pltpu.make_async_copy(v_in.at[pl.ds(2 * i, 2)], vbuf.at[pl.ds(2 * i, 2)], v_sem.at[i])
        for i in range(8)
    ]

    mesh_id = pl.DeviceIdType.MESH
    barrier = pltpu.get_barrier_semaphore()
    next_x = [((x + d) % X * Z + z, head) for d in (1, X - 1)]
    next_z = [(ctx_z(d), head) for d in (1, Z - 1)]
    partners = [(ctx, to) for to in (sib, up, down, far)] + next_z + next_x
    for to in partners:
        pl.semaphore_signal(barrier, 1, device_id=to, device_id_type=mesh_id)
    for cp in copies + v_copies:
        cp.start()
    pl.semaphore_wait(barrier, len(partners))

    def gather(src, buf, n):
        def g(i, a, b, to):
            return remote(a, b, gs_sem.at[n, i], gr_sem.at[n, i], head_to=to)

        def shard(h):
            return buf.at[pl.ds(2 * h, 2)]

        return [
            g(0, src, shard(head), sib),
            g(1, src, shard(head), up),
            g(2, src, shard(head), down),
            g(3, src, shard(head), far),
            g(4, shard(down), shard(down), sib),
            g(5, shard(up), shard(up), sib),
            g(6, shard(far), shard(far), sib),
        ]

    def step(copies, *pairs):
        for landed, started in pairs:
            copies[landed].wait_recv()
            copies[started].start()

    gk = gather(k_in, kbuf, 0)
    gq = gather(q_in, qbuf, 1)
    for i in (3, 1, 2, 0):
        gk[i].start()
    for to in next_z + next_x:
        pl.semaphore_signal(in_sem.at[0], 1, device_id=to, device_id_type=mesh_id)

    for cp in v_copies:
        cp.wait()

    @pl.loop(0, 8)
    def _(i):
        for odd in range(2):
            vt[i, :, odd * 128 : (odd + 1) * 128] = vbuf[2 * i + odd].T

    copies[0].wait()
    copies[1].wait()

    @pl.loop(0, 8)
    def _(i):
        r = rows[:, pl.ds(pl.multiple_of(i * 256, 256), 256)]
        ws = [jnp.zeros(r.shape, F32) for _ in range(4)]
        for cl in range(16):
            hit = r == cl
            ws = [jnp.where(hit, table[h, cl], w) for h, w in enumerate(ws)]
        for h, w in enumerate(ws):
            sh[i, pl.ds(16 * h, 10), :] = w / jnp.sum(w, axis=0, keepdims=True)

    pl.semaphore_wait(in_sem.at[0], 4)
    for d in (2, Z - 2):
        pl.semaphore_signal(
            in_sem.at[1], 1, device_id=(ctx_z(d), head), device_id_type=mesh_id
        )

    step(gk, (1, 4), (2, 5))
    for i in (3, 1, 2):
        gq[i].start()


    def states(h):
        g0 = nn(vt[h, :, :128], kbuf[2 * h])
        g1 = nn(vt[h, :, 128:], kbuf[2 * h + 1])
        lev1[h] = g0.astype(BF16)
        pairs[h] = (g0 + g1).reshape(8, CHUNK, 128)

    copies[2].wait()
    states(head)
    gk[0].wait_recv()
    states(sib)
    step(gk, (3, 6))
    gq[0].start()
    states(down)
    states(up)
    states(far)
    gk[4].wait_recv()
    states(down_s)
    gk[5].wait_recv()
    states(up_s)
    gk[6].wait_recv()
    states(far_s)
    pl.semaphore_wait(in_sem.at[1], 2)

    a2a = [
        remote(send.at[z_at(d)], recv.at[z], as_sem.at[d], ar_sem.at[d], ctx_to=ctx_z(d))
        for d in range(1, Z)
    ]

    def chunk_state(j):
        p = [pairs[h, j] for h in range(8)]
        for i in range(4):
            lev2[i, j] = p[2 * i].astype(BF16)
        p4 = [p[2 * i] + p[2 * i + 1] for i in range(4)]
        lev3[0, j] = p4[0].astype(BF16)
        lev3[1, j] = p4[2].astype(BF16)
        low = p4[0] + p4[1]
        lev4[j] = low.astype(BF16)
        send[j] = (low + p4[2] + p4[3]).astype(BF16)

    for d in (4, 3, 5, 2, 6, 1, 7):
        chunk_state(z_at(d))
        a2a[d - 1].start()
    chunk_state(z)
    recv[z] = send[z]

    z_next = remote(send, zst.at[0], zs_sem.at[0, 0], zr_sem.at[0, 0], ctx_to=ctx_z(1))

    @pl.when(z % 2 == 0)
    def _():
        z_next.start()

    causal = lax.broadcasted_iota(jnp.int32, (GROUP, GROUP), 0) >= lax.broadcasted_iota(
        jnp.int32, (GROUP, GROUP), 1
    )
    heads = [slice(h * GROUP, (h + 1) * GROUP) for h in range(4)]

    def share(i, level, h):
        return sh[i, 16 * h + level : 16 * h + level + 1, :]

    def add_far(i, state, level):
        f = nt(state, qbuf[pl.ds(2 * i, 2)].reshape(256, 128))
        for h in range(4):
            total[i, heads[h], :] += f[heads[h]] * share(i, level, h)

    def near(i):
        for odd in range(2):
            g = 2 * i + odd
            cols = slice(odd * GROUP, (odd + 1) * GROUP)
            q = qbuf[g]
            s = jnp.where(causal, nt(q, kbuf[g]), 0.0).astype(BF16)
            f0 = nt(vt[i, :, cols], s)
            if odd:
                f1 = nt(lev1[i], q)
            for h in range(4):
                t = f0[heads[h]] * share(i, 0, h)[:, cols]
                if odd:
                    t += f1[heads[h]] * share(i, 1, h)[:, cols]
                total[i, heads[h], cols] = t

        @pl.when(i % 2 == 1)
        def _():
            add_far(i, lev2[i // 2].reshape(512, 128), 2)

        @pl.when(i // 2 % 2 == 1)
        def _():
            add_far(i, lev3[i // 4].reshape(512, 128), 3)

        @pl.when(i // 4 == 1)
        def _():
            add_far(i, lev4[...].reshape(512, 128), 4)

    copies[3].wait()
    near(head)

    step(gq, (1, 4), (2, 5))

    @pl.loop(0, 2)
    def _(e):
        near((y + 1 + 2 * e) % Y * 2 + c)

    step(gq, (3, 6))

    for cp in a2a:
        cp.wait_recv()
    r = [recv[i].astype(F32) for i in range(8)]
    s01, s23, s45, s67 = (r[2 * i] + r[2 * i + 1] for i in range(4))
    s03 = s01 + s23
    row = s03 + s45 + s67
    row_f[...] = row
    row_b[...] = row.astype(BF16)

    def x_copy(to):
        return remote(row_b, row_r.at[x], xs_sem.at[to], xr_sem.at[x], ctx_to=to * Z + z)

    for to, sender in ((3, x < 2), (1, x == 0)):

        @pl.when(sender)
        def _():
            x_copy(to).start()

    pair6[0] = s01.astype(BF16)
    pair6[1] = s45.astype(BF16)
    half7[...] = s03.astype(BF16)

    def t_copy(to):
        ctx_to = (x + 1) % X * Z + to
        return remote(row_b, xst.at[0, z], bs_sem.at[0, to], br_sem.at[0, z], ctx_to=ctx_to)

    def z_copy(level, to):
        src = (None, pair6.at[to // 4], half7)[level]
        return remote(
            src, zst.at[level, z], zs_sem.at[level, to], zr_sem.at[level, z], ctx_to=x * Z + to
        )

    def direct(level, to):
        ok = z != to
        if level == 2:
            ok = jnp.logical_and(ok, z >= 4)
        return ok

    def z_send(level, to):
        @pl.when(direct(level, to))
        def _():
            z_copy(level, to).start()

    mate = jnp.maximum(z - 4, 0)

    def pass_on(to):
        slot = zst.at[2, mate]
        return remote(slot, slot, ps_sem.at[to - 4], zr_sem.at[2, mate], ctx_to=x * Z + to)

    high_z = range(4, 8)
    even = x % 2 == 0

    def t_send(*targets):
        @pl.when(even)
        def _():
            for to in targets:
                t_copy(to).start()

    @pl.when(z < 4)
    def _():
        z_copy(2, z + 4).start()

    t_send(0, 1)
    z_send(1, 2)
    z_send(1, 3)
    t_send(2, 3)
    z_send(2, 4)
    z_send(2, 5)
    t_send(4, 5)
    for to in (6, 7):
        z_send(2, to)
        z_send(1, to)
    t_send(6, 7)

    zst[1, z] = pair6[z // 4]
    zst[2, z] = half7[...]

    gq[0].wait_recv()
    near(far)
    near(sib)
    gq[4].wait_recv()
    near(down_s)

    def b_copy(to):
        ctx_to = jnp.where(x == 1, 2, x) * Z + to
        return remote(both, xst.at[1, z], bs_sem.at[1, to], br_sem.at[1, z], ctx_to=ctx_to)

    def b_send(to):
        @pl.when(jnp.logical_or(x == 1, z != to))
        def _():
            b_copy(to).start()

    def landed(sems, dst, sources, had=None):
        for j in sources:
            there = z == j
            if had is not None:
                there = jnp.logical_or(there, had == j)

            @pl.when(jnp.logical_not(there))
            def _():
                remote(half7, dst.at[j], sems.at[j], sems.at[j]).wait_recv()

    def x_wait(s):
        remote(row_b, row_r.at[s], xs_sem.at[s], xr_sem.at[s]).wait_recv()

    @pl.when(x == 1)
    def _():
        x_wait(0)
        both[...] = (row_r[0].astype(F32) + row_f[...]).astype(BF16)

    @pl.when(x == 3)
    def _():
        x_wait(0)
        x_wait(1)
        t = (row_r[0].astype(F32) + row_r[1].astype(F32)).astype(BF16)
        both[...] = t
        xst[1, z] = t

    @pl.when(x % 2 == 1)
    def _():
        for to in range(Z):
            b_send(to)

    gq[5].wait_recv()
    gq[6].wait_recv()

    @pl.loop(1, 3)
    def _(e):
        near((y + e) % Y * 2 + 1 - c)

    @pl.when(z >= 4)
    def _():
        remote(half7, zst.at[2, mate], zr_sem.at[2, mate], zr_sem.at[2, mate]).wait_recv()
        for to in high_z:

            @pl.when(z != to)
            def _():
                pass_on(to).start()

    def add_all(state, level):
        @pl.loop(0, 4)
        def _(m):
            for i in range(2):
                add_far(2 * m + i, state.reshape(512, 128), level)

    @pl.when(z % 2 == 1)
    def _():
        z_next.wait_recv()
        add_all(zst[0], 5)

    for level in (1, 2):

        @pl.when((z >> level) % 2 == 1)
        def _():
            landed(zr_sem.at[level], zst.at[level], range(Z), mate if level == 2 else None)
            add_all(zst[level], 5 + level)

    @pl.when(x % 2 == 1)
    def _():
        landed(br_sem.at[0], xst.at[0], range(Z))
        remote(half7, xst.at[0, z], br_sem.at[0, z], br_sem.at[0, z]).wait_recv()

    @pl.when(x == 3)
    def _():
        add_all(xst[0], 8)

    @pl.when(x >= 2)
    def _():
        landed(br_sem.at[1], xst.at[1], range(Z))

    @pl.when(x == 2)
    def _():
        remote(half7, xst.at[1, z], br_sem.at[1, z], br_sem.at[1, z]).wait_recv()

    for cp in gk + gq + a2a:
        cp.wait_send()

    @pl.when(z % 2 == 0)
    def _():
        z_next.wait_send()

    for to, sender in ((3, x < 2), (1, x == 0)):

        @pl.when(sender)
        def _():
            x_copy(to).wait_send()

    for level, targets in ((2, high_z), (1, (2, 3, 6, 7))):
        for to in targets:

            @pl.when(direct(level, to))
            def _():
                z_copy(level, to).wait_send()

    @pl.when(z < 4)
    def _():
        z_copy(2, z + 4).wait_send()

    @pl.when(z >= 4)
    def _():
        for to in high_z:

            @pl.when(z != to)
            def _():
                pass_on(to).wait_send()

    @pl.when(even)
    def _():
        for to in range(Z):
            t_copy(to).wait_send()

    @pl.when(x % 2 == 1)
    def _():
        for to in range(Z):

            @pl.when(jnp.logical_or(x == 1, z != to))
            def _():
                b_copy(to).wait_send()


def finish(qbuf, sh, total, xst, out, obuf, o_sem):
    def o_copy(i):
        g = pl.ds(2 * i, 2)
        return pltpu.make_async_copy(obuf.at[g], out.at[g], o_sem.at[i])

    def run(level):
        @pl.loop(0, 4)
        def _(m):
            for i in (2 * m, 2 * m + 1):
                if level:
                    state = xst[level - 8].reshape(512, 128)
                    f = nt(state, qbuf[pl.ds(2 * i, 2)].reshape(256, 128))
                for h in range(4):
                    rows = slice(h * GROUP, (h + 1) * GROUP)
                    t = total[i, rows, :]
                    if level:
                        lane = 16 * h + level
                        t += f[rows] * sh[i, lane : lane + 1, :]
                    obuf[pl.ds(2 * i, 2), :, rows] = t.astype(BF16).T.reshape(2, GROUP, GROUP)
                o_copy(i).start()

    x = lax.axis_index("ctx") // Z
    pl.when(x >= 2)(lambda: run(9))
    pl.when(x == 1)(lambda: run(8))
    pl.when(x == 0)(lambda: run(None))

    for i in range(8):
        o_copy(i).wait()


def local(queries, keys, values, tier_weight_rows, level_table):
    tokens, columns = values.shape
    groups = tokens // GROUP
    anywhere = pl.BlockSpec(memory_space=pl.ANY)
    vm = pltpu.VMEM
    kept = (
        vm((16, GROUP, 128), BF16),
        vm((8, 64, 256), F32),
        vm((8, 512, 256), F32),
        vm((2, 8, CHUNK, 128), BF16),
    )
    in_vmem = [pl.BlockSpec(memory_space=pltpu.VMEM)] * len(kept)
    parts = pl.pallas_call(
        kernel,
        out_shape=kept,
        in_specs=[pl.BlockSpec(memory_space=pltpu.MemorySpace.HBM)] * 5,
        out_specs=in_vmem,
        scratch_shapes=[
            vm((16, GROUP, 128), BF16),
            vm((16, GROUP, 512), BF16),
            vm((8, 512, 256), BF16),
            vm((10, 2048), jnp.int32),
            pltpu.SMEM((4, 16), F32),
            vm((8, 8, CHUNK, 128), F32),
            vm((8, 512, 128), BF16),
            vm((4, 8, CHUNK, 128), BF16),
            vm((2, 8, CHUNK, 128), BF16),
            vm((8, CHUNK, 128), BF16),
            vm((8, CHUNK, 128), BF16),
            vm((8, CHUNK, 128), BF16),
            vm((2, CHUNK, 128), BF16),
            vm((CHUNK, 128), BF16),
            vm((CHUNK, 128), F32),
            vm((CHUNK, 128), BF16),
            vm((2, CHUNK, 128), BF16),
            vm((CHUNK, 128), BF16),
            vm((3, 8, CHUNK, 128), BF16),
            DMA((4,)),
            DMA((8,)),
            DMA((2, 7)),
            DMA((2, 7)),
            DMA((8,)),
            DMA((8,)),
            DMA((3, 8)),
            DMA((3, 8)),
            DMA((4,)),
            DMA((2,)),
            DMA((2, 8)),
            DMA((2, 8)),
            DMA((4,)),
            pltpu.SemaphoreType.REGULAR((2,)),
        ],
        compiler_params=pltpu.CompilerParams(
            collective_id=0, has_side_effects=True, vmem_limit_bytes=24 * 2**20
        ),
    )(*(
        pltpu.with_memory_space_constraint(arg, pltpu.MemorySpace.HBM)
        for arg in (
            queries.reshape(2, GROUP, 128),
            keys.reshape(2, GROUP, 128),
            values.reshape(groups, GROUP, columns),
            tier_weight_rows,
            level_table.T,
        )
    ))
    out = pl.pallas_call(
        finish,
        out_shape=jax.ShapeDtypeStruct((groups, GROUP, columns), BF16),
        in_specs=in_vmem,
        out_specs=anywhere,
        scratch_shapes=[vm((groups, GROUP, columns), BF16), DMA((8,))],
        compiler_params=pltpu.CompilerParams(vmem_limit_bytes=12 * 2**20),
    )(*parts)
    return out.reshape(tokens, columns)


def solution(mesh):
    return jax.shard_map(
        local,
        mesh=mesh,
        in_specs=(
            P(("ctx", "head"), None),
            P(("ctx", "head"), None),
            P("ctx", "head"),
            P(None, "ctx"),
            P(None, "head"),
        ),
        out_specs=P("ctx", "head"),
        check_vma=False,
    )
```

```python
import functools

import jax
import jax.numpy as jnp
from jax import lax
from jax.experimental import pallas as pl
from jax.experimental.pallas import tpu as pltpu
from jax.sharding import PartitionSpec as P

GROUP = 128
X, Y, Z = 4, 4, 8
CHUNK = 64
F32, BF16 = jnp.float32, jnp.bfloat16
DMA = pltpu.SemaphoreType.DMA


def nt(a, b):
    return lax.dot_general(a, b, (((1,), (1,)), ((), ())), preferred_element_type=F32)


def nn(a, b):
    return jnp.dot(a, b, preferred_element_type=F32)


def kernel(
    q_in, k_in, v_in, rows_in, table_in,
    qbuf, sh, total, xst,
    kbuf, vbuf, vt, rows, table, pairs, lev1, lev2, lev3, lev4,
    send, recv, pair6, half7, row_f, row_b, row_r, both, zst,
    loc_sem, v_sem, gs_sem, gr_sem, as_sem, ar_sem, zs_sem, zr_sem,
    xs_sem, xr_sem, bs_sem, br_sem, ps_sem, in_sem,
):
    ctx = lax.axis_index("ctx")
    head = lax.axis_index("head")
    x, z = ctx // Z, ctx % Z
    y, c = head // 2, head % 2
    sib = y * 2 + 1 - c
    up = ((y + 1) % Y) * 2 + c
    down = ((y + 3) % Y) * 2 + c
    far = ((y + 2) % Y) * 2 + c
    up_s, down_s, far_s = (((y + d) % Y) * 2 + 1 - c for d in (1, 3, 2))

    def remote(src, dst, ss, rs, ctx_to=ctx, head_to=head):
        return pltpu.make_async_remote_copy(
            src, dst, ss, rs, device_id=(ctx_to, head_to), device_id_type=pl.DeviceIdType.MESH
        )

    def z_at(d):
        return (z + d) % Z

    def ctx_z(d):
        return x * Z + z_at(d)

    copies = [
        pltpu.make_async_copy(rows_in, rows, loc_sem.at[0]),
        pltpu.make_async_copy(table_in, table, loc_sem.at[1]),
        pltpu.make_async_copy(k_in, kbuf.at[pl.ds(2 * head, 2)], loc_sem.at[2]),
        pltpu.make_async_copy(q_in, qbuf.at[pl.ds(2 * head, 2)], loc_sem.at[3]),
    ]
    v_copies = [
        pltpu.make_async_copy(v_in.at[pl.ds(2 * i, 2)], vbuf.at[pl.ds(2 * i, 2)], v_sem.at[i])
        for i in range(8)
    ]

    mesh_id = pl.DeviceIdType.MESH
    barrier = pltpu.get_barrier_semaphore()
    next_x = [((x + d) % X * Z + z, head) for d in (1, X - 1)]
    next_z = [(ctx_z(d), head) for d in (1, Z - 1)]
    partners = [(ctx, to) for to in (sib, up, down, far)] + next_z + next_x
    for to in partners:
        pl.semaphore_signal(barrier, 1, device_id=to, device_id_type=mesh_id)
    for cp in copies + v_copies:
        cp.start()
    pl.semaphore_wait(barrier, len(partners))

    def gather(src, buf, n):
        def g(i, a, b, to):
            return remote(a, b, gs_sem.at[n, i], gr_sem.at[n, i], head_to=to)

        def shard(h):
            return buf.at[pl.ds(2 * h, 2)]

        return [
            g(0, src, shard(head), sib),
            g(1, src, shard(head), up),
            g(2, src, shard(head), down),
            g(3, src, shard(head), far),
            g(4, shard(down), shard(down), sib),
            g(5, shard(up), shard(up), sib),
            g(6, shard(far), shard(far), sib),
        ]

    def step(copies, *pairs):
        for landed, started in pairs:
            copies[landed].wait_recv()
            copies[started].start()

    gk = gather(k_in, kbuf, 0)
    gq = gather(q_in, qbuf, 1)
    for i in (3, 1, 2, 0):
        gk[i].start()
    for to in next_z + next_x:
        pl.semaphore_signal(in_sem.at[0], 1, device_id=to, device_id_type=mesh_id)

    for cp in v_copies:
        cp.wait()

    @pl.loop(0, 8)
    def _(i):
        for odd in range(2):
            vt[i, :, odd * 128 : (odd + 1) * 128] = vbuf[2 * i + odd].T

    copies[0].wait()
    copies[1].wait()

    @pl.loop(0, 8)
    def _(i):
        r = rows[:, pl.ds(pl.multiple_of(i * 256, 256), 256)]
        ws = [jnp.zeros(r.shape, F32) for _ in range(4)]
        for cl in range(16):
            hit = r == cl
            ws = [jnp.where(hit, table[h, cl], w) for h, w in enumerate(ws)]
        for h, w in enumerate(ws):
            sh[i, pl.ds(16 * h, 10), :] = w / jnp.sum(w, axis=0, keepdims=True)

    pl.semaphore_wait(in_sem.at[0], 4)
    for d in (2, Z - 2):
        pl.semaphore_signal(
            in_sem.at[1], 1, device_id=(ctx_z(d), head), device_id_type=mesh_id
        )

    step(gk, (1, 4), (2, 5))
    for i in (3, 1, 2):
        gq[i].start()


    def states(h):
        g0 = nn(vt[h, :, :128], kbuf[2 * h])
        g1 = nn(vt[h, :, 128:], kbuf[2 * h + 1])
        lev1[h] = g0.astype(BF16)
        pairs[h] = (g0 + g1).reshape(8, CHUNK, 128)

    copies[2].wait()
    states(head)
    gk[0].wait_recv()
    states(sib)
    step(gk, (3, 6))
    gq[0].start()
    states(down)
    states(up)
    states(far)
    gk[4].wait_recv()
    states(down_s)
    gk[5].wait_recv()
    states(up_s)
    gk[6].wait_recv()
    states(far_s)
    pl.semaphore_wait(in_sem.at[1], 2)

    a2a = [
        remote(send.at[z_at(d)], recv.at[z], as_sem.at[d], ar_sem.at[d], ctx_to=ctx_z(d))
        for d in range(1, Z)
    ]

    def chunk_state(j):
        p = [pairs[h, j] for h in range(8)]
        for i in range(4):
            lev2[i, j] = p[2 * i].astype(BF16)
        p4 = [p[2 * i] + p[2 * i + 1] for i in range(4)]
        lev3[0, j] = p4[0].astype(BF16)
        lev3[1, j] = p4[2].astype(BF16)
        low = p4[0] + p4[1]
        lev4[j] = low.astype(BF16)
        send[j] = (low + p4[2] + p4[3]).astype(BF16)

    for d in (4, 3, 5, 2, 6, 1, 7):
        chunk_state(z_at(d))
        a2a[d - 1].start()
    chunk_state(z)
    recv[z] = send[z]

    z_next = remote(send, zst.at[0], zs_sem.at[0, 0], zr_sem.at[0, 0], ctx_to=ctx_z(1))

    @pl.when(z % 2 == 0)
    def _():
        z_next.start()

    causal = lax.broadcasted_iota(jnp.int32, (GROUP, GROUP), 0) >= lax.broadcasted_iota(
        jnp.int32, (GROUP, GROUP), 1
    )
    heads = [slice(h * GROUP, (h + 1) * GROUP) for h in range(4)]

    def share(i, level, h):
        return sh[i, 16 * h + level : 16 * h + level + 1, :]

    def add_far(i, state, level):
        f = nt(state, qbuf[pl.ds(2 * i, 2)].reshape(256, 128))
        for h in range(4):
            total[i, heads[h], :] += f[heads[h]] * share(i, level, h)

    def near(i):
        for odd in range(2):
            g = 2 * i + odd
            cols = slice(odd * GROUP, (odd + 1) * GROUP)
            q = qbuf[g]
            s = jnp.where(causal, nt(q, kbuf[g]), 0.0).astype(BF16)
            f0 = nt(vt[i, :, cols], s)
            if odd:
                f1 = nt(lev1[i], q)
            for h in range(4):
                t = f0[heads[h]] * share(i, 0, h)[:, cols]
                if odd:
                    t += f1[heads[h]] * share(i, 1, h)[:, cols]
                total[i, heads[h], cols] = t

        @pl.when(i % 2 == 1)
        def _():
            add_far(i, lev2[i // 2].reshape(512, 128), 2)

        @pl.when(i // 2 % 2 == 1)
        def _():
            add_far(i, lev3[i // 4].reshape(512, 128), 3)

        @pl.when(i // 4 == 1)
        def _():
            add_far(i, lev4[...].reshape(512, 128), 4)

    copies[3].wait()
    near(head)

    step(gq, (1, 4), (2, 5))

    @pl.loop(0, 2)
    def _(e):
        near((y + 1 + 2 * e) % Y * 2 + c)

    step(gq, (3, 6))

    for cp in a2a:
        cp.wait_recv()
    r = [recv[i].astype(F32) for i in range(8)]
    s01, s23, s45, s67 = (r[2 * i] + r[2 * i + 1] for i in range(4))
    s03 = s01 + s23
    row = s03 + s45 + s67
    row_f[...] = row

    def x_copy(to):
        return remote(row_f, row_r.at[x], xs_sem.at[to], xr_sem.at[x], ctx_to=to * Z + z)

    for to, sender in ((3, x < 2), (1, x == 0)):

        @pl.when(sender)
        def _():
            x_copy(to).start()

    row_b[...] = row.astype(BF16)
    pair6[0] = s01.astype(BF16)
    pair6[1] = s45.astype(BF16)
    half7[...] = s03.astype(BF16)

    def t_copy(to):
        ctx_to = (x + 1) % X * Z + to
        return remote(row_b, xst.at[0, z], bs_sem.at[0, to], br_sem.at[0, z], ctx_to=ctx_to)

    def z_copy(level, to):
        src = (None, pair6.at[to // 4], half7)[level]
        return remote(
            src, zst.at[level, z], zs_sem.at[level, to], zr_sem.at[level, z], ctx_to=x * Z + to
        )

    def direct(level, to):
        ok = z != to
        if level == 2:
            ok = jnp.logical_and(ok, z >= 4)
        return ok

    def z_send(level, to):
        @pl.when(direct(level, to))
        def _():
            z_copy(level, to).start()

    mate = jnp.maximum(z - 4, 0)

    def pass_on(to):
        slot = zst.at[2, mate]
        return remote(slot, slot, ps_sem.at[to - 4], zr_sem.at[2, mate], ctx_to=x * Z + to)

    high_z = range(4, 8)
    even = x % 2 == 0

    def t_send(*targets):
        @pl.when(even)
        def _():
            for to in targets:
                t_copy(to).start()

    @pl.when(z < 4)
    def _():
        z_copy(2, z + 4).start()

    t_send(0, 1)
    z_send(1, 2)
    z_send(1, 3)
    t_send(2, 3)
    z_send(2, 4)
    z_send(2, 5)
    t_send(4, 5)
    for to in (6, 7):
        z_send(2, to)
        z_send(1, to)
    t_send(6, 7)

    zst[1, z] = pair6[z // 4]
    zst[2, z] = half7[...]

    gq[0].wait_recv()
    near(far)
    near(sib)
    gq[4].wait_recv()
    near(down_s)

    def b_copy(to):
        ctx_to = jnp.where(x == 1, 2, x) * Z + to
        return remote(both, xst.at[1, z], bs_sem.at[1, to], br_sem.at[1, z], ctx_to=ctx_to)

    def b_send(to):
        @pl.when(jnp.logical_or(x == 1, z != to))
        def _():
            b_copy(to).start()

    def landed(sems, dst, sources, had=None):
        for j in sources:
            there = z == j
            if had is not None:
                there = jnp.logical_or(there, had == j)

            @pl.when(jnp.logical_not(there))
            def _():
                remote(half7, dst.at[j], sems.at[j], sems.at[j]).wait_recv()

    def x_wait(s):
        remote(row_f, row_r.at[s], xs_sem.at[s], xr_sem.at[s]).wait_recv()

    @pl.when(x == 1)
    def _():
        x_wait(0)
        both[...] = (row_r[0] + row_f[...]).astype(BF16)

    @pl.when(x == 3)
    def _():
        x_wait(0)
        x_wait(1)
        t = (row_r[0] + row_r[1]).astype(BF16)
        both[...] = t
        xst[1, z] = t

    @pl.when(x % 2 == 1)
    def _():
        for to in range(Z):
            b_send(to)

    gq[5].wait_recv()
    gq[6].wait_recv()

    @pl.loop(1, 3)
    def _(e):
        near((y + e) % Y * 2 + 1 - c)

    @pl.when(z >= 4)
    def _():
        remote(half7, zst.at[2, mate], zr_sem.at[2, mate], zr_sem.at[2, mate]).wait_recv()
        for to in high_z:

            @pl.when(z != to)
            def _():
                pass_on(to).start()

    def add_all(state, level):
        @pl.loop(0, 4)
        def _(m):
            for i in range(2):
                add_far(2 * m + i, state.reshape(512, 128), level)

    @pl.when(z % 2 == 1)
    def _():
        z_next.wait_recv()
        add_all(zst[0], 5)

    for level in (1, 2):

        @pl.when((z >> level) % 2 == 1)
        def _():
            landed(zr_sem.at[level], zst.at[level], range(Z), mate if level == 2 else None)
            add_all(zst[level], 5 + level)

    @pl.when(x % 2 == 1)
    def _():
        landed(br_sem.at[0], xst.at[0], range(Z))
        remote(half7, xst.at[0, z], br_sem.at[0, z], br_sem.at[0, z]).wait_recv()

    @pl.when(x == 3)
    def _():
        add_all(xst[0], 8)

    @pl.when(x >= 2)
    def _():
        landed(br_sem.at[1], xst.at[1], range(Z))

    @pl.when(x == 2)
    def _():
        remote(half7, xst.at[1, z], br_sem.at[1, z], br_sem.at[1, z]).wait_recv()

    for cp in gk + gq + a2a:
        cp.wait_send()

    @pl.when(z % 2 == 0)
    def _():
        z_next.wait_send()

    for to, sender in ((3, x < 2), (1, x == 0)):

        @pl.when(sender)
        def _():
            x_copy(to).wait_send()

    for level, targets in ((2, high_z), (1, (2, 3, 6, 7))):
        for to in targets:

            @pl.when(direct(level, to))
            def _():
                z_copy(level, to).wait_send()

    @pl.when(z < 4)
    def _():
        z_copy(2, z + 4).wait_send()

    @pl.when(z >= 4)
    def _():
        for to in high_z:

            @pl.when(z != to)
            def _():
                pass_on(to).wait_send()

    @pl.when(even)
    def _():
        for to in range(Z):
            t_copy(to).wait_send()

    @pl.when(x % 2 == 1)
    def _():
        for to in range(Z):

            @pl.when(jnp.logical_or(x == 1, z != to))
            def _():
                b_copy(to).wait_send()


def finish(qbuf, sh, total, xst, out, obuf, o_sem):
    def o_copy(i):
        g = pl.ds(2 * i, 2)
        return pltpu.make_async_copy(obuf.at[g], out.at[g], o_sem.at[i])

    def run(level):
        @pl.loop(0, 2)
        def _(m):
            for i in (4 * m, 4 * m + 1, 4 * m + 2, 4 * m + 3):
                if level:
                    state = xst[level - 8].reshape(512, 128)
                    f = nt(state, qbuf[pl.ds(2 * i, 2)].reshape(256, 128))
                for h in range(4):
                    rows = slice(h * GROUP, (h + 1) * GROUP)
                    t = total[i, rows, :]
                    if level:
                        lane = 16 * h + level
                        t += f[rows] * sh[i, lane : lane + 1, :]
                    obuf[pl.ds(2 * i, 2), :, rows] = t.astype(BF16).T.reshape(2, GROUP, GROUP)
                o_copy(i).start()

    x = lax.axis_index("ctx") // Z
    pl.when(x >= 2)(lambda: run(9))
    pl.when(x == 1)(lambda: run(8))
    pl.when(x == 0)(lambda: run(None))

    for i in range(8):
        o_copy(i).wait()


def local(queries, keys, values, tier_weight_rows, level_table):
    tokens, columns = values.shape
    groups = tokens // GROUP
    anywhere = pl.BlockSpec(memory_space=pl.ANY)
    vm = pltpu.VMEM
    kept = (
        vm((16, GROUP, 128), BF16),
        vm((8, 64, 256), F32),
        vm((8, 512, 256), F32),
        vm((2, 8, CHUNK, 128), BF16),
    )
    in_vmem = [pl.BlockSpec(memory_space=pltpu.VMEM)] * len(kept)
    parts = pl.pallas_call(
        kernel,
        out_shape=kept,
        in_specs=[pl.BlockSpec(memory_space=pltpu.MemorySpace.HBM)] * 5,
        out_specs=in_vmem,
        scratch_shapes=[
            vm((16, GROUP, 128), BF16),
            vm((16, GROUP, 512), BF16),
            vm((8, 512, 256), BF16),
            vm((10, 2048), jnp.int32),
            pltpu.SMEM((4, 16), F32),
            vm((8, 8, CHUNK, 128), F32),
            vm((8, 512, 128), BF16),
            vm((4, 8, CHUNK, 128), BF16),
            vm((2, 8, CHUNK, 128), BF16),
            vm((8, CHUNK, 128), BF16),
            vm((8, CHUNK, 128), BF16),
            vm((8, CHUNK, 128), BF16),
            vm((2, CHUNK, 128), BF16),
            vm((CHUNK, 128), BF16),
            vm((CHUNK, 128), F32),
            vm((CHUNK, 128), BF16),
            vm((2, CHUNK, 128), F32),
            vm((CHUNK, 128), BF16),
            vm((3, 8, CHUNK, 128), BF16),
            DMA((4,)),
            DMA((8,)),
            DMA((2, 7)),
            DMA((2, 7)),
            DMA((8,)),
            DMA((8,)),
            DMA((3, 8)),
            DMA((3, 8)),
            DMA((4,)),
            DMA((2,)),
            DMA((2, 8)),
            DMA((2, 8)),
            DMA((4,)),
            pltpu.SemaphoreType.REGULAR((2,)),
        ],
        compiler_params=pltpu.CompilerParams(
            collective_id=0, has_side_effects=True, vmem_limit_bytes=24 * 2**20
        ),
    )(*(
        pltpu.with_memory_space_constraint(arg, pltpu.MemorySpace.HBM)
        for arg in (
            queries.reshape(2, GROUP, 128),
            keys.reshape(2, GROUP, 128),
            values.reshape(groups, GROUP, columns),
            tier_weight_rows,
            level_table.T,
        )
    ))
    out = pl.pallas_call(
        finish,
        out_shape=jax.ShapeDtypeStruct((groups, GROUP, columns), BF16),
        in_specs=in_vmem,
        out_specs=anywhere,
        scratch_shapes=[vm((groups, GROUP, columns), BF16), DMA((8,))],
        compiler_params=pltpu.CompilerParams(vmem_limit_bytes=12 * 2**20),
    )(*parts)
    return out.reshape(tokens, columns)


def solution(mesh):
    return jax.shard_map(
        local,
        mesh=mesh,
        in_specs=(
            P(("ctx", "head"), None),
            P(("ctx", "head"), None),
            P("ctx", "head"),
            P(None, "ctx"),
            P(None, "head"),
        ),
        out_specs=P("ctx", "head"),
        check_vma=False,
    )
```
